32 devices in a mesh: dp: 8 (over z, x), tensor: 4 (over y, core).
Axes of the slice: x: 2, y: 2, z: 4, core: 2. Of those that a mesh axis runs over, the one named last changes fastest.
Arguments:
- activations: bfloat16 [2048, 6144], P('dp'), may hold values from -6 to 6
- pre_act: bfloat16 [2048, 24576], P('dp', 'tensor'), may hold values from -8 to 8
- grad_act: bfloat16 [2048, 24576], P('dp', 'tensor'), may hold values from -6 to 6
- kept_weight: bfloat16 [4, 576, 128, 128], P('tensor', 'dp'), may hold values from -0.15625 to 0.15625
- block_cols: int32 [4, 576], P('tensor'), may hold values from 0 to 47, as said below
Outputs:
- weight_grad: bfloat16 [4, 576, 128, 128], P('tensor', 'dp')
- act_grad: bfloat16 [2048, 6144], P('dp')
The draws below stay inside these ranges and needn't reach their ends.
Inputs may be any that keep to these rules, and one draw needn't show every extreme that they name: `block_cols`: the kept blocks are listed block row by block row, 12 to a row; within one block row of one tensor index the 12 block columns are distinct.
All inputs are finite; a program needn't handle non-finite values.
Results may differ from the reference program's by a relative error of at most 0.0049.
Values may be sent and summed in bfloat16 or wider, within the bound.
No kernel may reach another device: no remote copies, remote signals or barrier semaphores. Data moves between devices by JAX's collectives and lax.ppermute only.
A program may use at most 256 MiB of HBM per device.

```python
import math
import jax
import jax.numpy as jnp
from jax import lax

D = 6144
FF = 24576
BLOCK = 128
TOKENS = 2048
PER_ROW = 12
KEPT = 576
N_TENSOR = 4


def draw_block_cols(key, part):
    blocks_q = FF // N_TENSOR // BLOCK
    blocks_d = D // BLOCK
    per_row = KEPT // blocks_d
    row_keys = jax.random.split(jax.random.fold_in(key, 11), N_TENSOR * blocks_d)

    def pick_row(row_key):
        return jax.random.permutation(row_key, blocks_q)[:per_row].astype(jnp.int32)
    picked = jax.vmap(pick_row)(row_keys)
    return picked.reshape(N_TENSOR, KEPT).astype(jnp.int32)


def steps_of(key, dims, cuts, low, high):
    def one(position, shards_of):
        heights = jax.random.uniform(jax.random.fold_in(jax.random.fold_in(key, 6), position), (shards_of,), jnp.float32, low / len(cuts), high / len(cuts))
        return jnp.repeat(jnp.exp(heights), dims[position] // shards_of).reshape((-1,) + (1,) * (len(dims) - position - 1))

    loudness = one(*cuts[0])
    for cut in cuts[1:]:
        loudness = loudness * one(*cut)
    return loudness


def noise(stream_key, extent, scale, most, cuts=(), kind=jnp.bfloat16):
    loudness = steps_of(stream_key, extent, cuts, -0.22, 0.18) if cuts else 1.0
    result = jax.random.normal(stream_key, extent, jnp.float32) * scale * loudness
    return jnp.minimum(jnp.maximum(result, -most), most).astype(kind)


def setup_inputs(seed: int = 0) -> dict:
    streams_of = jax.random.split(jax.random.key(seed), 6)
    return {
        "activations": noise(streams_of[0], (TOKENS, D), 1.0, 6.0, ((0, 8),)),
        "pre_act": noise(streams_of[1], (TOKENS, FF), 1.5, 8.0, ((0, 8), (1, 4))),
        "grad_act": noise(streams_of[2], (TOKENS, FF), 1.0, 6.0, ((0, 8), (1, 4))),
        "kept_weight": noise(streams_of[3], (N_TENSOR, KEPT, BLOCK, BLOCK), (PER_ROW * BLOCK) ** -0.5, 0.15625, ((0, 4), (1, 8))),
        "block_cols": draw_block_cols(jax.random.fold_in(streams_of[5], 71), 0),
    }


gelu_coef = math.sqrt(2.0 / math.pi)

def gelu_slope(pre_vals):
    pre_wide = pre_vals.astype(jnp.float32)
    inner_arg = gelu_coef * (pre_wide + 0.044715 * pre_wide ** 3)
    tanh_val = jnp.tanh(inner_arg)
    return 0.5 * (1.0 + tanh_val) + 0.5 * pre_wide * (1.0 - tanh_val ** 2) * gelu_coef * (1.0 + 3.0 * 0.044715 * pre_wide ** 2)

def reference(activations, pre_act, grad_act, kept_weight, block_cols):
    tokens_all = activations.shape[0]
    width_dev = FF // N_TENSOR
    blocks_d = D // BLOCK
    per_row = KEPT // blocks_d
    act_blocks = activations.reshape(tokens_all, blocks_d, BLOCK)
    grad_scale = 1.0 / math.sqrt(tokens_all)

    def shard_work(shard_index):
        pre_vals = lax.dynamic_slice_in_dim(pre_act, shard_index * width_dev, width_dev, 1)
        upstream = lax.dynamic_slice_in_dim(grad_act, shard_index * width_dev, width_dev, 1)
        hidden_grad = (upstream.astype(jnp.float32) * gelu_slope(pre_vals)).astype(jnp.bfloat16)
        grad_blocks = hidden_grad.reshape(tokens_all, width_dev // BLOCK, BLOCK)
        col_table = lax.dynamic_index_in_dim(block_cols, shard_index, 0, keepdims=False).reshape(blocks_d, per_row)
        weights = lax.dynamic_index_in_dim(kept_weight, shard_index, 0, keepdims=False).reshape(blocks_d, per_row, BLOCK, BLOCK)

        def per_block_row(row_index):
            col_pick = lax.dynamic_index_in_dim(col_table, row_index, 0, keepdims=False)
            grad_row = jnp.take(grad_blocks, col_pick, axis=1).astype(jnp.float32)
            act_row = lax.dynamic_index_in_dim(act_blocks, row_index, 1, keepdims=False).astype(jnp.float32)
            weight_row = lax.dynamic_index_in_dim(weights, row_index, 0, keepdims=False).astype(jnp.float32)
            block_grad = (jnp.einsum('ta,tkf->kaf', act_row, grad_row) * grad_scale).astype(jnp.bfloat16)
            act_part = jnp.einsum('tkf,kdf->td', grad_row, weight_row)
            return (act_part, block_grad)
        act_parts, block_terms = lax.map(per_block_row, jnp.arange(blocks_d, dtype=jnp.int32))
        return (act_parts, block_terms.reshape(KEPT, BLOCK, BLOCK))

    def accumulate(running, shard_index):
        shard_out = shard_work(shard_index)
        return (running + shard_out[0], shard_out[1])
    zero_total = jnp.zeros((blocks_d, tokens_all, BLOCK), jnp.float32)
    summed, weight_grad = lax.scan(accumulate, zero_total, jnp.arange(N_TENSOR, dtype=jnp.int32))
    act_grad = jnp.transpose(summed, (1, 0, 2)).reshape(tokens_all, D).astype(jnp.bfloat16)
    return (weight_grad, act_grad)
```

```python
import functools
import math

import jax
import jax.numpy as jnp
from jax import lax
from jax.experimental import pallas as pl
from jax.experimental.pallas import tpu as pltpu
from jax.sharding import PartitionSpec as P


gelu_coef = math.sqrt(2.0 / math.pi)


def gelu_slope(pre_vals):
    pre_wide = pre_vals.astype(jnp.float32)
    inner_arg = gelu_coef * (pre_wide + 0.044715 * pre_wide**3)
    tanh_val = jnp.tanh(inner_arg)
    return 0.5 * (1.0 + tanh_val) + 0.5 * pre_wide * (1.0 - tanh_val**2) * gelu_coef * (
        1.0 + 3.0 * 0.044715 * pre_wide**2
    )


def hidden_gradient(pre_act, grad_act):
    return (grad_act.astype(jnp.float32) * gelu_slope(pre_act)).astype(jnp.bfloat16)


def group_of(amount):
    chosen = 1
    for divisor in range(1, 9):
        if amount % divisor == 0:
            chosen = divisor
    return chosen


def local_any(activations, pre_act, grad_act, kept_weight, block_cols):
    block = kept_weight.shape[-1]
    tok_count, width = activations.shape
    blocks_d = width // block
    dp_size = lax.axis_size("dp")
    grad_scale = 1.0 / math.sqrt(tok_count * dp_size)
    act_blocks = activations.reshape(tok_count, blocks_d, block)
    hidden_grad = hidden_gradient(pre_act, grad_act)
    grad_blocks = hidden_grad.reshape(tok_count, -1, block)
    col_ids = block_cols[0]
    kept_all = col_ids.shape[0]
    per_row = kept_all // blocks_d
    col_table = col_ids.reshape(blocks_d, per_row)
    row_group = group_of(blocks_d)
    group_count = blocks_d // row_group
    gathered = lax.all_gather(kept_weight, "dp", axis=1, tiled=True)
    whole_weights = gathered[0].reshape(blocks_d, per_row, block, block)

    def with_terms(group_index):
        first_row = group_index * row_group
        col_pick = lax.dynamic_slice_in_dim(col_table, first_row, row_group, 0).reshape(-1)
        grad_group = jnp.take(grad_blocks, col_pick, axis=1).reshape(
            tok_count, row_group, per_row, block
        )
        weight_group = lax.dynamic_slice_in_dim(whole_weights, first_row, row_group, 0)
        act_part = jnp.einsum(
            "trkf,rkdf->trd", grad_group, weight_group, preferred_element_type=jnp.float32
        )
        act_group = lax.dynamic_slice_in_dim(act_blocks, first_row, row_group, 1)
        block_term = (
            jnp.einsum("tra,trkf->rkaf", act_group, grad_group, preferred_element_type=jnp.float32)
            * grad_scale
        )
        return (act_part, block_term)

    act_parts, block_terms = lax.map(with_terms, jnp.arange(group_count, dtype=jnp.int32))
    summed = lax.psum_scatter(
        block_terms.reshape(kept_all, block, block), "dp", scatter_dimension=0, tiled=True
    )
    weight_grad = summed.astype(jnp.bfloat16).reshape(1, -1, block, block)
    partial_value = jnp.transpose(act_parts, (1, 0, 2, 3)).reshape(tok_count, width)
    act_grad = lax.psum(partial_value, "tensor").astype(jnp.bfloat16)
    return (weight_grad, act_grad)


PAIR = 2


def weight_term_kernel(
    per_row, rows, grad_scale, place_ref, cols_ref, mine_ref, theirs_ref, hid_ref, hid2_ref, out_ref
):
    step = pl.program_id(0)
    unit = step // rows
    row = step % rows
    block = mine_ref.shape[1]

    @pl.when(place_ref[1 + 2 * unit] > 0)
    def _():
        first = ((place_ref[2 + 2 * unit] * PAIR + place_ref[0]) * rows + row) * per_row
        act = jnp.concatenate([mine_ref[...], theirs_ref[...]], axis=0)
        group = 4 if per_row % 4 == 0 else 1
        act_t = act.T

        @pl.loop(0, per_row // group)
        def _(part):
            start = part * group
            spans = [
                pl.ds(pl.multiple_of(cols_ref[first + start + k] * block, block), block)
                for k in range(group)
            ]
            hid = jnp.concatenate(
                [
                    jnp.concatenate([hid_ref[:, span] for span in spans], axis=1),
                    jnp.concatenate([hid2_ref[:, span] for span in spans], axis=1),
                ],
                axis=0,
            )
            term = (
                lax.dot_general(
                    act_t, hid, (((1,), (0,)), ((), ())), preferred_element_type=jnp.float32
                )
                * grad_scale
            )
            for k in range(group):
                out_ref[start + k] = term[:, k * block : (k + 1) * block].astype(out_ref.dtype)


def weight_terms(units, x_place, cols, mine, theirs, hid, hid2, rows, per_row, grad_scale, kind):
    tok, block = mine.shape[0], mine.shape[1] * per_row // cols.shape[0]
    place = jnp.stack(
        [x_place] + [v.astype(jnp.int32) for pair in units for v in pair]
    ).astype(jnp.int32)
    count = len(units)

    def mine_map(step, place_ref, cols_ref):
        unit = place_ref[2 + 2 * (step // rows)]
        return (0, (unit * PAIR + place_ref[0]) * rows + step % rows)

    def theirs_map(step, place_ref, cols_ref):
        return (0, place_ref[2 + 2 * (step // rows)] * rows + step % rows)

    whole = pl.BlockSpec(hid.shape, lambda step, *_: (0, 0))
    kept = rows * per_row
    flops = 2 * count * kept * 2 * tok * block * block
    return pl.pallas_call(
        functools.partial(weight_term_kernel, per_row, rows, grad_scale),
        out_shape=jax.ShapeDtypeStruct((count * kept, block, block), kind),
        grid_spec=pltpu.PrefetchScalarGridSpec(
            num_scalar_prefetch=2,
            grid=(count * rows,),
            in_specs=[
                pl.BlockSpec((tok, block), mine_map),
                pl.BlockSpec((tok, block), theirs_map),
                whole,
                whole,
            ],
            out_specs=pl.BlockSpec((per_row, block, block), lambda step, *_: (step, 0, 0)),
        ),
        cost_estimate=pl.CostEstimate(
            flops=flops, bytes_accessed=4 * tok * hid.shape[1] + 4 * count * kept * block * block, transcendentals=0
        ),
        name="weight_terms",
    )(place, cols, mine, theirs, hid, hid2)


def act_kernel(per_row, rows, reach, place_ref, cols_ref, hid_ref, hid2_ref, *refs):
    sources = refs[: 2 * reach + 1]
    mine_ref, theirs_ref, held, sems = refs[2 * reach + 1 :]
    step = pl.program_id(0)
    steps = pl.num_programs(0)
    block = held.shape[-1]
    tok = hid_ref.shape[0]

    def copy_of(source, at_row, slot):
        return pltpu.make_async_copy(
            source.at[pl.ds(at_row * per_row, per_row)], held.at[slot], sems.at[slot]
        )

    def fetch(at_step):
        away = place_ref[2] + at_step // rows - place_ref[1]
        for index, source in enumerate(sources):
            distance = index if index <= reach else reach - index

            @pl.when(away == distance)
            def _():
                copy_of(source, at_step % rows, at_step % 2).start()

    @pl.when(step == 0)
    def _():
        fetch(0)

    @pl.when(step + 1 < steps)
    def _():
        fetch(step + 1)

    slot = step % 2
    copy_of(sources[0], 0, slot).wait()
    unit = place_ref[2] + step // rows
    first = ((unit * PAIR + place_ref[0]) * rows + step % rows) * per_row
    spans = [
        pl.ds(pl.multiple_of(cols_ref[first + k] * block, block), block) for k in range(per_row)
    ]
    hid = jnp.concatenate(
        [
            jnp.concatenate([hid_ref[:, span] for span in spans], axis=1),
            jnp.concatenate([hid2_ref[:, span] for span in spans], axis=1),
        ],
        axis=0,
    )
    weight = jnp.concatenate([held[slot, k] for k in range(per_row)], axis=1)
    part = lax.dot_general(
        hid, weight, (((1,), (1,)), ((), ())), preferred_element_type=jnp.float32
    )
    mine_ref[...] = part[:tok].astype(mine_ref.dtype)
    theirs_ref[...] = part[tok:].astype(theirs_ref.dtype)


def act_partials(x_place, z_place, first_unit, count, cols, hid, hid2, sources, rows, per_row):
    block = sources[0].shape[-1]
    tok = hid.shape[0]
    reach = (len(sources) - 1) // 2
    place = jnp.stack([x_place, z_place, first_unit]).astype(jnp.int32)
    whole = pl.BlockSpec(hid.shape, lambda step, *_: (0, 0))
    out = pl.BlockSpec((tok, block), lambda step, *_: (0, step))
    shape = jax.ShapeDtypeStruct((tok, count * rows * block), jnp.bfloat16)
    kept = count * rows * per_row
    return pl.pallas_call(
        functools.partial(act_kernel, per_row, rows, reach),
        out_shape=(shape, shape),
        grid_spec=pltpu.PrefetchScalarGridSpec(
            num_scalar_prefetch=2,
            grid=(count * rows,),
            in_specs=[whole, whole] + [pl.BlockSpec(memory_space=pl.ANY)] * len(sources),
            out_specs=[out, out],
            scratch_shapes=[
                pltpu.VMEM((2, per_row, block, block), jnp.bfloat16),
                pltpu.SemaphoreType.DMA((2,)),
            ],
        ),
        cost_estimate=pl.CostEstimate(
            flops=4 * kept * tok * block * block,
            bytes_accessed=4 * tok * hid.shape[1] + 2 * kept * block * block,
            transcendentals=0,
        ),
        name="act_partials",
    )(place, cols, hid, hid2, *sources)


def put_kernel(place_ref, mine_ref, other_ref, *refs):
    out_ref = refs[-1]
    turn = pl.program_id(0) % 2

    @pl.when(turn == 0)
    def _():
        out_ref[...] = mine_ref[...]

    @pl.when(turn == 1)
    def _():
        out_ref[...] = other_ref[...]


def put_units(x_place, parity, first_unit, count, mine, other, whole, width):
    tok = mine.shape[0]
    span = mine.shape[1] // count
    place = jnp.stack([(x_place + parity) % 2, first_unit]).astype(jnp.int32)

    def out_map(step, place_ref):
        return (0, (place_ref[1] + step // 2) * PAIR + (place_ref[0] + step) % 2)

    part = pl.BlockSpec((tok, span), lambda step, *_: (0, step // 2))
    given = [] if whole is None else [whole]
    return pl.pallas_call(
        put_kernel,
        out_shape=jax.ShapeDtypeStruct((tok, width), jnp.bfloat16),
        grid_spec=pltpu.PrefetchScalarGridSpec(
            num_scalar_prefetch=1,
            grid=(2 * count,),
            in_specs=[part, part] + [pl.BlockSpec(memory_space=pl.ANY)] * len(given),
            out_specs=pl.BlockSpec((tok, span), out_map),
        ),
        input_output_aliases={3: 0} if given else {},
        cost_estimate=pl.CostEstimate(
            flops=0, bytes_accessed=8 * tok * span * count, transcendentals=0
        ),
        name="put_units",
    )(place, mine, other, *given)


def local_line(activations, pre_act, grad_act, kept_weight, block_cols):
    block = kept_weight.shape[-1]
    tok, width = activations.shape
    dp_size, tensor_size = lax.axis_size("dp"), lax.axis_size("tensor")
    line = dp_size // PAIR
    kept = kept_weight.shape[1]
    cols = block_cols[0]
    per_row = cols.shape[0] // (width // block)
    rows = kept // per_row
    span = rows * block
    grad_scale = 1.0 / math.sqrt(tok * dp_size)
    place = lax.axis_index("dp")
    z_place, x_place = place // PAIR, place % PAIR
    t_place = lax.axis_index("tensor")

    def along(value, steps, keep):
        return lax.ppermute(
            value,
            "dp",
            [
                (z * PAIR + x, (z + steps) * PAIR + x)
                for z in range(line)
                for x in range(PAIR)
                if 0 <= z + steps < line and keep(z)
            ],
        )

    def across(value):
        return lax.ppermute(value, "dp", [(d, d ^ 1) for d in range(dp_size)])

    def partner(value, bit):
        return lax.ppermute(value, "tensor", [(t, t ^ bit) for t in range(tensor_size)])

    own_weight = kept_weight[0]
    from_left, from_right = [], []
    going_right = going_left = own_weight
    for step in range(1, line):
        going_right = along(going_right, 1, lambda z, step=step: z >= step - 1)
        going_left = along(going_left, -1, lambda z, step=step: line - 1 - z >= step - 1)
        from_left.append(going_right)
        from_right.append(going_left)

    share = tok // tensor_size
    mine_share = lax.dynamic_slice_in_dim(activations, t_place * share, share, 0)
    asked = [
        jnp.concatenate(
            [mine_share[:, (u * PAIR + x) * span : (u * PAIR + x + 1) * span] for u in range(line)],
            axis=1,
        )
        for x in range(PAIR)
    ]
    piece = across(jnp.where(x_place == 0, asked[1], asked[0]))
    pieces = {0: piece}
    bit = tensor_size // 2
    while bit:
        held = sorted(pieces)
        got = partner(jnp.stack([pieces[k] for k in held]), bit)
        for index, k in enumerate(held):
            pieces[k ^ bit] = got[index]
        bit //= 2
    their_acts = jnp.zeros((tok, line * span), activations.dtype)
    for k, value in pieces.items():
        their_acts = lax.dynamic_update_slice_in_dim(
            their_acts, value, (t_place ^ k) * share, 0
        )

    hid = hidden_gradient(pre_act, grad_act)
    hid2 = across(hid)

    terms = functools.partial(
        weight_terms,
        x_place=x_place,
        cols=cols,
        mine=activations,
        theirs=their_acts,
        hid=hid,
        hid2=hid2,
        rows=rows,
        per_row=per_row,
        grad_scale=grad_scale,
    )
    sum_right = sum_left = None
    for step in range(1, line):
        off = line - step
        units = [
            (z_place + off < line, jnp.minimum(z_place + off, line - 1)),
            (z_place - off >= 0, jnp.maximum(z_place - off, 0)),
        ]
        if step == line - 1:
            units.append((z_place >= 0, z_place))
        both = terms(units, kind=jnp.bfloat16 if step == 1 else jnp.float32)
        right, left = both[:kept], both[kept : 2 * kept]
        if step > 1:
            right = (right + sum_right.astype(jnp.float32)).astype(jnp.bfloat16)
            left = (left + sum_left.astype(jnp.float32)).astype(jnp.bfloat16)
        sum_right = along(right, 1, lambda z, off=off: z + off < line)
        sum_left = along(left, -1, lambda z, off=off: z - off >= 0)
    weight_grad = (
        both[2 * kept :] + sum_right.astype(jnp.float32) + sum_left.astype(jnp.float32)
    ).astype(jnp.bfloat16)

    half = line // 2
    act_grad = None
    for stage in range(2):
        side = (z_place // half) if stage == 0 else 1 - z_place // half
        reach = half - 1 if stage == 0 else line - 1
        sources = [own_weight] + from_right[:reach] + from_left[:reach]
        mine, theirs = act_partials(
            x_place, z_place, side * half, half, cols, hid, hid2, sources, rows, per_row
        )
        parts = jnp.stack([mine, across(theirs)])
        parts = (
            parts.astype(jnp.float32) + partner(parts, 1).astype(jnp.float32)
        ).astype(jnp.bfloat16)
        mine_half = lax.dynamic_index_in_dim(parts, t_place % 2, 0, keepdims=False)
        bit = 2
        while bit < tensor_size:
            mine_half = (
                mine_half.astype(jnp.float32) + partner(mine_half, bit).astype(jnp.float32)
            ).astype(jnp.bfloat16)
            bit *= 2
        other_half = partner(mine_half, 1)
        act_grad = put_units(
            x_place, t_place % 2, side * half, half, mine_half, other_half, act_grad, width
        )
    return (weight_grad[None], act_grad)


def fits_line(mesh, activations, kept_weight, block_cols):
    dp_size, tensor_size = mesh.shape["dp"], mesh.shape["tensor"]
    block = kept_weight.shape[-1]
    kept_all = kept_weight.shape[1]
    per_row = kept_all // (activations.shape[1] // block)
    return (
        dp_size % (2 * PAIR) == 0
        and tensor_size >= 2
        and tensor_size & (tensor_size - 1) == 0
        and kept_all % (dp_size * per_row) == 0
        and activations.shape[0] % (dp_size * tensor_size * 16) == 0
        and activations.shape[0] // dp_size <= 512
    )


def solution(mesh):
    def whole(activations, pre_act, grad_act, kept_weight, block_cols):
        fits = fits_line(mesh, activations, kept_weight, block_cols)
        return jax.shard_map(
            local_line if fits else local_any,
            mesh=mesh,
            in_specs=(
                P("dp", None),
                P("dp", "tensor"),
                P("dp", "tensor"),
                P("tensor", "dp", None, None),
                P("tensor", None),
            ),
            out_specs=(P("tensor", "dp", None, None), P("dp", None)),
            check_vma=False,
        )(activations, pre_act, grad_act, kept_weight, block_cols)

    return whole
```

```python
import functools
import math

import jax
import jax.numpy as jnp
from jax import lax
from jax.experimental import pallas as pl
from jax.experimental.pallas import tpu as pltpu
from jax.sharding import PartitionSpec as P


gelu_coef = math.sqrt(2.0 / math.pi)


def gelu_slope(pre_vals):
    pre_wide = pre_vals.astype(jnp.float32)
    inner_arg = gelu_coef * (pre_wide + 0.044715 * pre_wide**3)
    tanh_val = jnp.tanh(inner_arg)
    return 0.5 * (1.0 + tanh_val) + 0.5 * pre_wide * (1.0 - tanh_val**2) * gelu_coef * (
        1.0 + 3.0 * 0.044715 * pre_wide**2
    )


def hidden_gradient(pre_act, grad_act):
    return (grad_act.astype(jnp.float32) * gelu_slope(pre_act)).astype(jnp.bfloat16)


def group_of(amount):
    chosen = 1
    for divisor in range(1, 9):
        if amount % divisor == 0:
            chosen = divisor
    return chosen


def local_any(activations, pre_act, grad_act, kept_weight, block_cols):
    block = kept_weight.shape[-1]
    tok_count, width = activations.shape
    blocks_d = width // block
    dp_size = lax.axis_size("dp")
    grad_scale = 1.0 / math.sqrt(tok_count * dp_size)
    act_blocks = activations.reshape(tok_count, blocks_d, block)
    hidden_grad = hidden_gradient(pre_act, grad_act)
    grad_blocks = hidden_grad.reshape(tok_count, -1, block)
    col_ids = block_cols[0]
    kept_all = col_ids.shape[0]
    per_row = kept_all // blocks_d
    col_table = col_ids.reshape(blocks_d, per_row)
    row_group = group_of(blocks_d)
    group_count = blocks_d // row_group
    gathered = lax.all_gather(kept_weight, "dp", axis=1, tiled=True)
    whole_weights = gathered[0].reshape(blocks_d, per_row, block, block)

    def with_terms(group_index):
        first_row = group_index * row_group
        col_pick = lax.dynamic_slice_in_dim(col_table, first_row, row_group, 0).reshape(-1)
        grad_group = jnp.take(grad_blocks, col_pick, axis=1).reshape(
            tok_count, row_group, per_row, block
        )
        weight_group = lax.dynamic_slice_in_dim(whole_weights, first_row, row_group, 0)
        act_part = jnp.einsum(
            "trkf,rkdf->trd", grad_group, weight_group, preferred_element_type=jnp.float32
        )
        act_group = lax.dynamic_slice_in_dim(act_blocks, first_row, row_group, 1)
        block_term = (
            jnp.einsum("tra,trkf->rkaf", act_group, grad_group, preferred_element_type=jnp.float32)
            * grad_scale
        )
        return (act_part, block_term)

    act_parts, block_terms = lax.map(with_terms, jnp.arange(group_count, dtype=jnp.int32))
    summed = lax.psum_scatter(
        block_terms.reshape(kept_all, block, block), "dp", scatter_dimension=0, tiled=True
    )
    weight_grad = summed.astype(jnp.bfloat16).reshape(1, -1, block, block)
    partial_value = jnp.transpose(act_parts, (1, 0, 2, 3)).reshape(tok_count, width)
    act_grad = lax.psum(partial_value, "tensor").astype(jnp.bfloat16)
    return (weight_grad, act_grad)


SIDE, NEAR, FAR = 1, 2, 4
SETS = (0, SIDE, FAR, FAR | SIDE)
CHUNKS = 4


def columns_of(chunk_refs, spans):
    return jnp.concatenate(
        [jnp.concatenate([ref[:, span] for span in spans], axis=1) for ref in chunk_refs], axis=0
    )


def spans_of(cols_ref, first, count, block):
    return [
        pl.ds(pl.multiple_of(cols_ref[first + k] * block, block), block) for k in range(count)
    ]


def weight_term_kernel(
    per_row, rows, first_row, grad_scale, act_count, hid_count, place_ref, cols_ref, *refs
):
    act_refs, hid_refs = refs[:act_count], refs[act_count : act_count + hid_count]
    acc_refs, out_ref = refs[act_count + hid_count : -1], refs[-1]
    row = first_row + pl.program_id(0)
    block = act_refs[0].shape[1]
    first = (place_ref[0] * rows + row) * per_row
    act_t = jnp.concatenate([ref[...] for ref in act_refs], axis=0).T
    group = 4 if per_row % 4 == 0 else 1

    @pl.loop(0, per_row // group)
    def _(part):
        start = part * group
        hid = columns_of(hid_refs, spans_of(cols_ref, first + start, group, block))
        term = (
            lax.dot_general(
                act_t, hid, (((1,), (0,)), ((), ())), preferred_element_type=jnp.float32
            )
            * grad_scale
        )
        for k in range(group):
            value = term[:, k * block : (k + 1) * block]
            for acc_ref in acc_refs:
                value = value + acc_ref[start + k]
            out_ref[start + k] = value.astype(out_ref.dtype)


def weight_terms(place, cols, acts, hids, acc, first_row, count, rows, per_row, grad_scale, kind):
    tok = acts[0][0].shape[0]
    block = acts[0][0].shape[1] * per_row // cols.shape[0] if acts[0][1] is None else acts[0][2]

    def act_spec(kind_of):
        if kind_of is None:
            return pl.BlockSpec(
                (tok, block), lambda s, place_ref, _: (0, place_ref[0] * rows + first_row + s)
            )
        return pl.BlockSpec(
            (tok, block),
            lambda s, place_ref, _: (0, (kind_of * 2 + place_ref[1]) * rows + first_row + s),
        )

    chunks = [chunk for hid in hids for chunk in hid]
    accs = [] if acc is None else [acc]
    unit_spec = pl.BlockSpec((per_row, block, block), lambda s, *_: (s, 0, 0))
    acc_spec = pl.BlockSpec((per_row, block, block), lambda s, *_: (first_row + s, 0, 0))
    kept = count * per_row
    return pl.pallas_call(
        functools.partial(
            weight_term_kernel, per_row, rows, first_row, grad_scale, len(acts), len(chunks)
        ),
        out_shape=jax.ShapeDtypeStruct((kept, block, block), kind),
        grid_spec=pltpu.PrefetchScalarGridSpec(
            num_scalar_prefetch=2,
            grid=(count,),
            in_specs=[act_spec(entry[1]) for entry in acts]
            + [pl.BlockSpec(chunk.shape, lambda s, *_: (0, 0)) for chunk in chunks]
            + [acc_spec] * len(accs),
            out_specs=unit_spec,
        ),
        cost_estimate=pl.CostEstimate(
            flops=2 * kept * len(hids) * tok * block * block,
            bytes_accessed=2 * len(hids) * tok * chunks[0].shape[1] + 8 * kept * block * block,
            transcendentals=0,
        ),
        name="weight_terms",
    )(place, cols, *[entry[0] for entry in acts], *chunks, *accs)


def act_kernel(per_row, rows, set_count, hid_count, place_ref, cols_ref, *refs):
    hid_refs = refs[:hid_count]
    sources = refs[hid_count : hid_count + 2]
    outs = refs[hid_count + 2 : -2]
    held, sems = refs[-2:]
    step = pl.program_id(0)
    steps = pl.num_programs(0)
    block = held.shape[-1]

    def near_of(at_step):
        return jnp.where(at_step < rows, place_ref[2], 1 - place_ref[2])

    def copy_of(source, at_row, slot):
        return pltpu.make_async_copy(
            source.at[pl.ds(at_row * per_row, per_row)], held.at[slot], sems.at[slot]
        )

    def fetch(at_step):
        for index, source in enumerate(sources):

            @pl.when((near_of(at_step) == place_ref[1]) == (index == 0))
            def _():
                copy_of(source, at_step % rows, at_step % 2).start()

    @pl.when(step == 0)
    def _():
        fetch(0)

    @pl.when(step + 1 < steps)
    def _():
        fetch(step + 1)

    slot = step % 2
    copy_of(sources[0], 0, slot).wait()
    first = ((place_ref[0] + NEAR * near_of(step)) * rows + step % rows) * per_row
    hid = columns_of(hid_refs, spans_of(cols_ref, first, per_row, block))
    weight = jnp.concatenate([held[slot, k] for k in range(per_row)], axis=1)
    part = lax.dot_general(
        hid, weight, (((1,), (1,)), ((), ())), preferred_element_type=jnp.float32
    ).astype(jnp.bfloat16)
    tok = part.shape[0] // set_count

    @pl.when(step < rows)
    def _():
        for k in range(set_count):
            outs[2 * k][...] = part[k * tok : (k + 1) * tok]

    @pl.when(step >= rows)
    def _():
        for k in range(set_count):
            outs[2 * k + 1][...] = part[k * tok : (k + 1) * tok]


def act_partials(place, cols, hids, weights, rows, per_row):
    block = weights[0].shape[-1]
    chunks = [chunk for hid in hids for chunk in hid]
    tok = sum(chunk.shape[0] for chunk in hids[0])
    keep = pl.BlockSpec((tok, block), lambda s, *_: (0, jnp.minimum(s, rows - 1)))
    give = pl.BlockSpec((tok, block), lambda s, *_: (0, jnp.maximum(s - rows, 0)))
    shape = jax.ShapeDtypeStruct((tok, rows * block), jnp.bfloat16)
    kept = 2 * rows * per_row
    return pl.pallas_call(
        functools.partial(act_kernel, per_row, rows, len(hids), len(chunks)),
        out_shape=(shape,) * (2 * len(hids)),
        grid_spec=pltpu.PrefetchScalarGridSpec(
            num_scalar_prefetch=2,
            grid=(2 * rows,),
            in_specs=[pl.BlockSpec(chunk.shape, lambda s, *_: (0, 0)) for chunk in chunks]
            + [pl.BlockSpec(memory_space=pl.ANY)] * 2,
            out_specs=[keep, give] * len(hids),
            scratch_shapes=[
                pltpu.VMEM((2, per_row, block, block), jnp.bfloat16),
                pltpu.SemaphoreType.DMA((2,)),
            ],
        ),
        cost_estimate=pl.CostEstimate(
            flops=2 * kept * len(hids) * tok * block * block,
            bytes_accessed=2 * len(hids) * tok * chunks[0].shape[1] + 2 * kept * block * block,
            transcendentals=0,
        ),
        name="act_partials",
    )(place, cols, *chunks, *weights)


def put_kernel(place_ref, *refs):
    ins, out_ref = refs[:-1], refs[-1]
    span = ins[0].shape[1]
    for index, ref in enumerate(ins):
        out_ref[:, pl.ds(pl.multiple_of(place_ref[index] * span, span), span)] = ref[...]


def put_units(units, arrays, width):
    tok = arrays[0].shape[0]
    return pl.pallas_call(
        put_kernel,
        out_shape=jax.ShapeDtypeStruct((tok, width), jnp.bfloat16),
        grid_spec=pltpu.PrefetchScalarGridSpec(
            num_scalar_prefetch=1,
            grid=(1,),
            in_specs=[pl.BlockSpec(array.shape, lambda s, *_: (0, 0)) for array in arrays],
            out_specs=pl.BlockSpec((tok, width), lambda s, *_: (0, 0)),
        ),
        cost_estimate=pl.CostEstimate(
            flops=0, bytes_accessed=4 * tok * width, transcendentals=0
        ),
        name="put_units",
    )(jnp.stack(units).astype(jnp.int32), *arrays)


def add_up(left, right):
    return (left.astype(jnp.float32) + right.astype(jnp.float32)).astype(jnp.bfloat16)


def after(value, *others):
    return lax.optimization_barrier((value, *others))[0]


def local_bits(activations, pre_act, grad_act, kept_weight, block_cols):
    block = kept_weight.shape[-1]
    tok, width = activations.shape
    dp_size, tensor_size = lax.axis_size("dp"), lax.axis_size("tensor")
    kept = kept_weight.shape[1]
    cols = block_cols[0]
    per_row = cols.shape[0] // (width // block)
    rows = kept // per_row
    span = rows * block
    grad_scale = 1.0 / math.sqrt(tok * dp_size)
    place = lax.axis_index("dp")
    side, near, far = place % 2, (place // NEAR) % 2, place // FAR
    t_place = lax.axis_index("tensor")
    core = t_place % 2

    def swap(value, bits):
        return lax.ppermute(value, "dp", [(d, d ^ bits) for d in range(dp_size)])

    def partner(value, bit):
        return lax.ppermute(value, "tensor", [(t, t ^ bit) for t in range(tensor_size)])

    share = tok // tensor_size
    mine_share = lax.dynamic_slice_in_dim(activations, t_place * share, share, 0)

    def share_for(bits):
        wanted = (place ^ bits) & (FAR | SIDE)
        options = [
            jnp.concatenate(
                [
                    mine_share[:, (base + NEAR * j) * span : (base + NEAR * j + 1) * span]
                    for j in range(2)
                ],
                axis=1,
            )
            for base in SETS
        ]
        chosen = options[0]
        for base, option in zip(SETS[1:], options[1:]):
            chosen = jnp.where(wanted == base, option, chosen)
        return chosen

    shares = [swap(share_for(bits), bits) for bits in SETS[1:]]

    part = tok // CHUNKS
    hid_own, hid_side, hid_far = [], [], []
    for k in range(CHUNKS):
        rows_of = slice(k * part, (k + 1) * part)
        hid_own.append(hidden_gradient(pre_act[rows_of], grad_act[rows_of]))
        hid_far.append(swap(hid_own[k], FAR))
        hid_side.append(swap(hid_own[k], SIDE))
    own_weight = kept_weight[0]
    near_weight = swap(own_weight, NEAR)
    hid_both = [swap(chunk, SIDE) for chunk in hid_far]

    pieces = {0: jnp.concatenate(shares, axis=1)}
    bit = tensor_size // 2
    while bit:
        held = sorted(pieces)
        got = partner(jnp.concatenate([pieces[k] for k in held], axis=0), bit)
        for index, k in enumerate(held):
            pieces[k ^ bit] = got[index * share : (index + 1) * share]
        bit //= 2
    their_acts = jnp.zeros((tok, 3 * 2 * span), activations.dtype)
    for k, value in pieces.items():
        their_acts = lax.dynamic_update_slice_in_dim(
            their_acts, value, (t_place ^ k) * share, 0
        )
    own_acts = (activations, None)
    set_acts = [(their_acts, s, block) for s in range(3)]

    near_place = jnp.stack([place ^ NEAR, 1 - near]).astype(jnp.int32)
    own_place = jnp.stack([place, near]).astype(jnp.int32)
    act_place = jnp.stack([place & (FAR | SIDE), near, core]).astype(jnp.int32)
    terms = functools.partial(
        weight_terms, cols=cols, rows=rows, per_row=per_row, grad_scale=grad_scale
    )
    early = functools.partial(
        terms,
        acts=[own_acts, set_acts[0]],
        hids=[hid_own, hid_side],
        acc=None,
        first_row=0,
        count=rows,
        kind=jnp.float32,
    )

    def reduced(keep, give):
        half = add_up(keep, partner(give, 1))
        bit = 2
        while bit < tensor_size:
            half = add_up(half, partner(half, bit))
            bit *= 2
        return half

    near_sum = early(near_place)
    own_sum = early(own_place)
    weights = (own_weight, near_weight)
    first_acts = act_partials(act_place, cols, [hid_own, hid_side], weights, rows, per_row)
    near_sum = terms(
        near_place, acts=[set_acts[1]], hids=[hid_far], acc=near_sum, first_row=0, count=rows,
        kind=jnp.float32,
    )
    far_acts = act_partials(act_place, cols, [hid_far], weights, rows, per_row)
    sent = []
    cuts = 2 if rows % 2 == 0 else 1
    for k in range(cuts):
        sent.append(
            terms(
                near_place, acts=[set_acts[2]], hids=[hid_both], acc=near_sum,
                first_row=k * (rows // cuts), count=rows // cuts, kind=jnp.bfloat16,
            )
        )
    came = [swap(value, NEAR) for value in sent]
    both_acts = act_partials(act_place, cols, [hid_both], weights, rows, per_row)
    own_sum = terms(
        own_place, acts=[set_acts[1], set_acts[2]], hids=[hid_far, hid_both], acc=own_sum,
        first_row=0, count=rows, kind=jnp.float32,
    )
    weight_grad = (own_sum + jnp.concatenate(came, axis=0).astype(jnp.float32)).astype(
        jnp.bfloat16
    )

    keeps = [first_acts[0], first_acts[2], far_acts[0], both_acts[0]]
    gives = [first_acts[1], first_acts[3], far_acts[1], both_acts[1]]
    mine, units = [], []
    for bits, keep, give in zip(SETS, keeps, gives):
        half = reduced(keep, give)
        mine.append(half if bits == 0 else swap(half, bits))
        units.append(((place & (FAR | SIDE)) ^ bits) + NEAR * core)
    other = [partner(half, 1) for half in mine]
    act_grad = put_units(units + [unit ^ NEAR for unit in units], mine + other, width)
    return (weight_grad[None], act_grad)


def fits_bits(mesh, activations, kept_weight, block_cols):
    dp_size, tensor_size = mesh.shape["dp"], mesh.shape["tensor"]
    block = kept_weight.shape[-1]
    kept_all = kept_weight.shape[1]
    per_row = kept_all // (activations.shape[1] // block)
    return (
        dp_size == 2 * FAR
        and tensor_size >= 2
        and tensor_size & (tensor_size - 1) == 0
        and kept_all % (dp_size * per_row) == 0
        and activations.shape[0] % (dp_size * tensor_size * 16) == 0
        and activations.shape[0] % (dp_size * CHUNKS * 16) == 0
        and activations.shape[0] // dp_size <= 512
    )


def solution(mesh):
    def whole(activations, pre_act, grad_act, kept_weight, block_cols):
        fits = fits_bits(mesh, activations, kept_weight, block_cols)
        return jax.shard_map(
            local_bits if fits else local_any,
            mesh=mesh,
            in_specs=(
                P("dp", None),
                P("dp", "tensor"),
                P("dp", "tensor"),
                P("tensor", "dp", None, None),
                P("tensor", None),
            ),
            out_specs=(P("tensor", "dp", None, None), P("dp", None)),
            check_vma=False,
        )(activations, pre_act, grad_act, kept_weight, block_cols)

    return whole
```

```python
import functools
import math

import jax
import jax.numpy as jnp
from jax import lax
from jax.experimental import pallas as pl
from jax.experimental.pallas import tpu as pltpu
from jax.sharding import PartitionSpec as P


gelu_coef = math.sqrt(2.0 / math.pi)


def gelu_slope(pre_vals):
    pre_wide = pre_vals.astype(jnp.float32)
    inner_arg = gelu_coef * (pre_wide + 0.044715 * pre_wide**3)
    tanh_val = jnp.tanh(inner_arg)
    return 0.5 * (1.0 + tanh_val) + 0.5 * pre_wide * (1.0 - tanh_val**2) * gelu_coef * (
        1.0 + 3.0 * 0.044715 * pre_wide**2
    )


def hidden_gradient(pre_act, grad_act):
    return (grad_act.astype(jnp.float32) * gelu_slope(pre_act)).astype(jnp.bfloat16)


def group_of(amount):
    chosen = 1
    for divisor in range(1, 9):
        if amount % divisor == 0:
            chosen = divisor
    return chosen


def local_any(activations, pre_act, grad_act, kept_weight, block_cols):
    block = kept_weight.shape[-1]
    tok_count, width = activations.shape
    blocks_d = width // block
    dp_size = lax.axis_size("dp")
    grad_scale = 1.0 / math.sqrt(tok_count * dp_size)
    act_blocks = activations.reshape(tok_count, blocks_d, block)
    hidden_grad = hidden_gradient(pre_act, grad_act)
    grad_blocks = hidden_grad.reshape(tok_count, -1, block)
    col_ids = block_cols[0]
    kept_all = col_ids.shape[0]
    per_row = kept_all // blocks_d
    col_table = col_ids.reshape(blocks_d, per_row)
    row_group = group_of(blocks_d)
    group_count = blocks_d // row_group
    gathered = lax.all_gather(kept_weight, "dp", axis=1, tiled=True)
    whole_weights = gathered[0].reshape(blocks_d, per_row, block, block)

    def with_terms(group_index):
        first_row = group_index * row_group
        col_pick = lax.dynamic_slice_in_dim(col_table, first_row, row_group, 0).reshape(-1)
        grad_group = jnp.take(grad_blocks, col_pick, axis=1).reshape(
            tok_count, row_group, per_row, block
        )
        weight_group = lax.dynamic_slice_in_dim(whole_weights, first_row, row_group, 0)
        act_part = jnp.einsum(
            "trkf,rkdf->trd", grad_group, weight_group, preferred_element_type=jnp.float32
        )
        act_group = lax.dynamic_slice_in_dim(act_blocks, first_row, row_group, 1)
        block_term = (
            jnp.einsum("tra,trkf->rkaf", act_group, grad_group, preferred_element_type=jnp.float32)
            * grad_scale
        )
        return (act_part, block_term)

    act_parts, block_terms = lax.map(with_terms, jnp.arange(group_count, dtype=jnp.int32))
    summed = lax.psum_scatter(
        block_terms.reshape(kept_all, block, block), "dp", scatter_dimension=0, tiled=True
    )
    weight_grad = summed.astype(jnp.bfloat16).reshape(1, -1, block, block)
    partial_value = jnp.transpose(act_parts, (1, 0, 2, 3)).reshape(tok_count, width)
    act_grad = lax.psum(partial_value, "tensor").astype(jnp.bfloat16)
    return (weight_grad, act_grad)


SIDE, NEAR, FAR = 1, 2, 4
SETS = (0, SIDE, FAR, FAR | SIDE)
CHUNKS = (6, 5, 3, 2)


def columns_of(chunk_refs, spans):
    return jnp.concatenate(
        [jnp.concatenate([ref[:, span] for span in spans], axis=1) for ref in chunk_refs], axis=0
    )


def spans_of(cols_ref, first, count, block):
    return [
        pl.ds(pl.multiple_of(cols_ref[first + k] * block, block), block) for k in range(count)
    ]


def weight_term_kernel(
    per_row, rows, first_row, grad_scale, act_count, hid_count, place_ref, cols_ref, *refs
):
    act_refs, hid_refs = refs[:act_count], refs[act_count : act_count + hid_count]
    acc_refs, out_ref = refs[act_count + hid_count : -1], refs[-1]
    step_rows = out_ref.shape[0] // per_row
    block = out_ref.shape[1]
    group = 4 if per_row % 4 == 0 else 1

    @pl.loop(0, step_rows)
    def _(step_row):
        row = first_row + pl.program_id(0) * step_rows + step_row
        first = (place_ref[0] * rows + row) * per_row
        lanes = pl.ds(pl.multiple_of(row * block, block), block)
        act_t = jnp.concatenate([ref[:, lanes] for ref in act_refs], axis=0).T
        for part in range(per_row // group):
            start = part * group
            hid = columns_of(hid_refs, spans_of(cols_ref, first + start, group, block))
            term = (
                lax.dot_general(
                    act_t, hid, (((1,), (0,)), ((), ())), preferred_element_type=jnp.float32
                )
                * grad_scale
            )
            for k in range(group):
                value = term[:, k * block : (k + 1) * block]
                at = step_row * per_row + start + k
                for acc_ref in acc_refs:
                    value = value + acc_ref[at]
                out_ref[at] = value.astype(out_ref.dtype)


def weight_terms(
    place, cols, acts, hids, acc, first_row, count, rows, per_row, block, grad_scale, kind
):
    tok = acts[0][0].shape[0]
    step_rows = next(k for k in (3, 2, 1) if count % k == 0)

    def act_spec(kind_of):
        if kind_of is None:
            return pl.BlockSpec((tok, rows * block), lambda s, place_ref, _: (0, place_ref[0]))
        return pl.BlockSpec(
            (tok, rows * block), lambda s, place_ref, _: (0, kind_of * 2 + place_ref[1])
        )

    chunks = [chunk for hid in hids for chunk in hid]
    accs = [] if acc is None else [acc]
    unit_spec = pl.BlockSpec((step_rows * per_row, block, block), lambda s, *_: (s, 0, 0))
    acc_spec = pl.BlockSpec(
        (step_rows * per_row, block, block), lambda s, *_: (first_row // step_rows + s, 0, 0)
    )
    kept = count * per_row
    return pl.pallas_call(
        functools.partial(
            weight_term_kernel, per_row, rows, first_row, grad_scale, len(acts), len(chunks)
        ),
        out_shape=jax.ShapeDtypeStruct((kept, block, block), kind),
        grid_spec=pltpu.PrefetchScalarGridSpec(
            num_scalar_prefetch=2,
            grid=(count // step_rows,),
            in_specs=[act_spec(entry[1]) for entry in acts]
            + [pl.BlockSpec(chunk.shape, lambda s, *_: (0, 0)) for chunk in chunks]
            + [acc_spec] * len(accs),
            out_specs=unit_spec,
        ),
        cost_estimate=pl.CostEstimate(
            flops=2 * kept * len(hids) * tok * block * block,
            bytes_accessed=2 * len(hids) * tok * chunks[0].shape[1] + 8 * kept * block * block,
            transcendentals=0,
        ),
        name="weight_terms",
    )(place, cols, *[entry[0] for entry in acts], *chunks, *accs)


def act_kernel(per_row, rows, set_count, hid_count, place_ref, cols_ref, *refs):
    hid_refs = refs[:hid_count]
    sources = refs[hid_count : hid_count + 2]
    outs = refs[hid_count + 2 : -2]
    held, sems = refs[-2:]
    unit = pl.program_id(0)
    block = held.shape[-1]
    near = jnp.where(unit == 0, place_ref[2], 1 - place_ref[2])

    def copy_of(source, into):
        return pltpu.make_async_copy(source, held.at[into], sems.at[into])

    @pl.when(unit == 0)
    def _():
        for index, source in enumerate(sources):
            @pl.when(place_ref[2] == place_ref[1])
            def _():
                copy_of(source, index).start()

            @pl.when(place_ref[2] != place_ref[1])
            def _():
                copy_of(source, 1 - index).start()

    copy_of(sources[0], unit).wait()

    @pl.loop(0, rows)
    def _(row):
        first = ((place_ref[0] + NEAR * near) * rows + row) * per_row
        hid = columns_of(hid_refs, spans_of(cols_ref, first, per_row, block))
        weight = jnp.concatenate([held[unit, row * per_row + k] for k in range(per_row)], axis=1)
        part = lax.dot_general(
            hid, weight, (((1,), (1,)), ((), ())), preferred_element_type=jnp.float32
        ).astype(jnp.bfloat16)
        tok = part.shape[0] // set_count
        lanes = pl.ds(pl.multiple_of(row * block, block), block)

        @pl.when(unit == 0)
        def _():
            for k in range(set_count):
                outs[2 * k][:, lanes] = part[k * tok : (k + 1) * tok]

        @pl.when(unit == 1)
        def _():
            for k in range(set_count):
                outs[2 * k + 1][:, lanes] = part[k * tok : (k + 1) * tok]


def act_partials(place, cols, hids, weights, rows, per_row):
    block = weights[0].shape[-1]
    chunks = [chunk for hid in hids for chunk in hid]
    tok = sum(chunk.shape[0] for chunk in hids[0])
    out = pl.BlockSpec((tok, rows * block), lambda s, *_: (0, 0))
    shape = jax.ShapeDtypeStruct((tok, rows * block), jnp.bfloat16)
    kept = 2 * rows * per_row
    return pl.pallas_call(
        functools.partial(act_kernel, per_row, rows, len(hids), len(chunks)),
        out_shape=(shape,) * (2 * len(hids)),
        grid_spec=pltpu.PrefetchScalarGridSpec(
            num_scalar_prefetch=2,
            grid=(2,),
            in_specs=[pl.BlockSpec(chunk.shape, lambda s, *_: (0, 0)) for chunk in chunks]
            + [pl.BlockSpec(memory_space=pl.ANY)] * 2,
            out_specs=[out] * (2 * len(hids)),
            scratch_shapes=[
                pltpu.VMEM((2, rows * per_row, block, block), jnp.bfloat16),
                pltpu.SemaphoreType.DMA((2,)),
            ],
        ),
        cost_estimate=pl.CostEstimate(
            flops=2 * kept * len(hids) * tok * block * block,
            bytes_accessed=2 * len(hids) * tok * chunks[0].shape[1] + 2 * kept * block * block,
            transcendentals=0,
        ),
        name="act_partials",
    )(place, cols, *chunks, *weights)


def put_kernel(count, place_ref, *refs):
    ins, out_ref, sems = refs[:count], refs[-2], refs[-1]
    copies = []
    for index, ref in enumerate(ins):
        tok, span = ref.shape
        into = out_ref.at[
            pl.ds(pl.multiple_of(place_ref[count + index] * tok, tok), tok),
            pl.ds(pl.multiple_of(place_ref[index] * span, span), span),
        ]
        copies.append(pltpu.make_async_copy(ref, into, sems.at[index]))
        copies[-1].start()
    for copy in copies:
        copy.wait()


def put_units(units, parts, arrays, whole, shape):
    given = [] if whole is None else [whole]
    count = len(arrays)
    return pl.pallas_call(
        functools.partial(put_kernel, count),
        out_shape=jax.ShapeDtypeStruct(shape, jnp.bfloat16),
        grid_spec=pltpu.PrefetchScalarGridSpec(
            num_scalar_prefetch=1,
            grid=(1,),
            in_specs=[pl.BlockSpec(array.shape, lambda s, *_: (0, 0)) for array in arrays]
            + [pl.BlockSpec(memory_space=pl.ANY)] * len(given),
            out_specs=pl.BlockSpec(memory_space=pl.ANY),
            scratch_shapes=[pltpu.SemaphoreType.DMA((count,))],
        ),
        input_output_aliases={count + 1: 0} if given else {},
        cost_estimate=pl.CostEstimate(
            flops=0, bytes_accessed=4 * count * arrays[0].size, transcendentals=0
        ),
        name="put_units",
    )(jnp.stack(units + parts).astype(jnp.int32), *arrays, *given)


def add_up(left, right):
    return (left.astype(jnp.float32) + right.astype(jnp.float32)).astype(jnp.bfloat16)


def after(value, *others):
    return lax.optimization_barrier((value, *others))[0]


def local_bits(*arrays):
    return local_bits_body(*arrays)


def local_bits_body(activations, pre_act, grad_act, kept_weight, block_cols):
    block = kept_weight.shape[-1]
    tok, width = activations.shape
    dp_size, tensor_size = lax.axis_size("dp"), lax.axis_size("tensor")
    kept = kept_weight.shape[1]
    cols = block_cols[0]
    per_row = cols.shape[0] // (width // block)
    rows = kept // per_row
    span = rows * block
    grad_scale = 1.0 / math.sqrt(tok * dp_size)
    place = lax.axis_index("dp")
    near = (place // NEAR) % 2
    t_place = lax.axis_index("tensor")
    core = t_place % 2

    def swap(value, bits):
        return lax.ppermute(value, "dp", [(d, d ^ bits) for d in range(dp_size)])

    def partner(value, bit):
        return lax.ppermute(value, "tensor", [(t, t ^ bit) for t in range(tensor_size)])

    hid_own, hid_side, hid_far = [], [], []
    cut = 0
    for part in CHUNKS:
        rows_of = slice(cut, cut + part * tok // sum(CHUNKS))
        cut = rows_of.stop
        pre_part = after(pre_act[rows_of], *hid_own[-1:])
        index = len(hid_own)
        hid_own.append(hidden_gradient(pre_part, grad_act[rows_of]))
        if not hid_far:
            hid_far.append(swap(hid_own[0], FAR))
        hid_side.append(swap(hid_own[-1], SIDE))

    share = tok // tensor_size
    mine_share = lax.dynamic_slice_in_dim(activations, t_place * share, share, 0)
    mine_share = after(mine_share, hid_own[-1])

    def share_for(bits):
        wanted = (place ^ bits) & (FAR | SIDE)
        options = [
            jnp.concatenate(
                [
                    mine_share[:, (base + NEAR * j) * span : (base + NEAR * j + 1) * span]
                    for j in range(2)
                ],
                axis=1,
            )
            for base in SETS
        ]
        chosen = options[0]
        for base, option in zip(SETS[1:], options[1:]):
            chosen = jnp.where(wanted == base, option, chosen)
        return chosen

    shares = [swap(share_for(bits), bits) for bits in SETS[1:]]
    own_weight = kept_weight[0]
    near_weight = swap(after(own_weight, hid_own[-1]), NEAR)
    pieces = {0: jnp.concatenate(shares, axis=1)}
    bit = tensor_size // 2
    while bit:
        held = sorted(pieces)
        got = partner(jnp.concatenate([pieces[k] for k in held], axis=0), bit)
        for index, k in enumerate(held):
            pieces[k ^ bit] = got[index * share : (index + 1) * share]
        bit //= 2
    their_acts = jnp.zeros((tok, 3 * 2 * span), activations.dtype)
    for k, value in pieces.items():
        their_acts = lax.dynamic_update_slice_in_dim(
            their_acts, value, (t_place ^ k) * share, 0
        )
    own_acts = (activations, None)
    set_acts = [(their_acts, s) for s in range(3)]

    near_place = jnp.stack([place ^ NEAR, 1 - near]).astype(jnp.int32)
    own_place = jnp.stack([place, near]).astype(jnp.int32)
    act_place = jnp.stack([place & (FAR | SIDE), near, core]).astype(jnp.int32)
    terms = functools.partial(
        weight_terms,
        cols=cols,
        first_row=0,
        count=rows,
        rows=rows,
        per_row=per_row,
        block=block,
        grad_scale=grad_scale,
    )
    first_terms = functools.partial(
        terms, acts=[own_acts, set_acts[0]], hids=[hid_own, hid_side], acc=None, kind=jnp.float32
    )
    weights = (own_weight, near_weight)

    def acts_of(hids, *others):
        return act_partials(after(act_place, *others), cols, hids, weights, rows, per_row)

    def core_sum(keep, give):
        return add_up(keep, partner(give, 1))

    def rest_sum(half, first_bit):
        bit = first_bit
        while bit < tensor_size:
            half = add_up(half, partner(half, bit))
            bit *= 2
        return half

    hid_both = [swap(hid_far[0], SIDE)]
    hid_far.append(swap(after(hid_own[1], hid_far[0]), FAR))
    near_sum = first_terms(after(near_place, hid_far[1]))
    own_sum = first_terms(after(own_place, near_sum))
    hid_both.append(swap(hid_far[1], SIDE))
    hid_far.append(swap(after(hid_own[2], hid_far[1]), FAR))
    third = after(hid_far[2], own_sum)
    hid_both.append(swap(third, SIDE))
    hid_far.append(swap(after(hid_own[3], third), FAR))
    first_acts = acts_of([hid_own, hid_side], third)
    halves = [rest_sum(core_sum(first_acts[2 * k], first_acts[2 * k + 1]), 2) for k in range(2)]
    fourth = after(hid_far[3], *halves)
    hid_both.append(swap(fourth, SIDE))
    far_acts = acts_of([hid_far], fourth)
    far_core = core_sum(far_acts[0], far_acts[1])

    sent = terms(
        after(near_place, far_core),
        acts=[set_acts[1], set_acts[2]],
        hids=[hid_far, hid_both],
        acc=near_sum,
        kind=jnp.bfloat16,
    )
    came = swap(sent, NEAR)
    both_acts = acts_of([hid_both], sent)
    both_core = core_sum(both_acts[0], both_acts[1])
    halves.append(rest_sum(far_core, 2))

    turn = (t_place // 2) % 2
    cut = tok // 2
    quarter = add_up(
        lax.dynamic_slice_in_dim(both_core, turn * cut, cut, 0),
        partner(lax.dynamic_slice_in_dim(both_core, (1 - turn) * cut, cut, 0), 2),
    )
    quarter = swap(rest_sum(quarter, 4), FAR | SIDE)
    quarters = [quarter, partner(quarter, 2)]

    own_sum = terms(
        after(own_place, both_core),
        acts=[set_acts[1], set_acts[2]],
        hids=[hid_far, hid_both],
        acc=own_sum,
        kind=jnp.float32,
    )
    weight_grad = (own_sum + came.astype(jnp.float32)).astype(jnp.bfloat16)

    unit = (place & (FAR | SIDE)) + NEAR * core
    mine = [halves[0], swap(halves[1], SIDE), swap(halves[2], FAR)]
    other = [partner(half, 1) for half in mine]
    units = [unit ^ bits for bits in SETS[:3]]
    whole = put_units(
        units + [u ^ NEAR for u in units], [core * 0] * 6, mine + other, None, activations.shape
    )
    last = unit ^ SETS[3]
    act_grad = put_units(
        [last, last, last ^ NEAR, last ^ NEAR],
        [turn, 1 - turn] * 2,
        quarters + [partner(value, 1) for value in quarters],
        whole,
        activations.shape,
    )
    return (weight_grad[None], act_grad)


def fits_bits(mesh, activations, kept_weight):
    dp_size, tensor_size = mesh.shape["dp"], mesh.shape["tensor"]
    block = kept_weight.shape[-1]
    kept_all = kept_weight.shape[1]
    per_row = kept_all // (activations.shape[1] // block)
    return (
        dp_size == 2 * FAR
        and tensor_size >= 4
        and tensor_size & (tensor_size - 1) == 0
        and kept_all % (dp_size * per_row) == 0
        and activations.shape[0] % (dp_size * tensor_size * 16) == 0
        and activations.shape[0] % (dp_size * sum(CHUNKS) * 16) == 0
        and activations.shape[0] // dp_size <= 512
    )


def solution(mesh):
    def whole(activations, pre_act, grad_act, kept_weight, block_cols):
        fits = fits_bits(mesh, activations, kept_weight)
        return jax.shard_map(
            local_bits if fits else local_any,
            mesh=mesh,
            in_specs=(
                P("dp", None),
                P("dp", "tensor"),
                P("dp", "tensor"),
                P("tensor", "dp", None, None),
                P("tensor", None),
            ),
            out_specs=(P("tensor", "dp", None, None), P("dp", None)),
            check_vma=False,
        )(activations, pre_act, grad_act, kept_weight, block_cols)

    return whole
```

```python
import functools
import math

import jax
import jax.numpy as jnp
from jax import lax
from jax.experimental import pallas as pl
from jax.experimental.pallas import tpu as pltpu
from jax.sharding import PartitionSpec as P


gelu_coef = math.sqrt(2.0 / math.pi)


def gelu_slope(pre_vals):
    pre_wide = pre_vals.astype(jnp.float32)
    inner_arg = gelu_coef * (pre_wide + 0.044715 * pre_wide**3)
    tanh_val = jnp.tanh(inner_arg)
    return 0.5 * (1.0 + tanh_val) + 0.5 * pre_wide * (1.0 - tanh_val**2) * gelu_coef * (
        1.0 + 3.0 * 0.044715 * pre_wide**2
    )


def hidden_gradient(pre_act, grad_act):
    return (grad_act.astype(jnp.float32) * gelu_slope(pre_act)).astype(jnp.bfloat16)


def group_of(amount):
    chosen = 1
    for divisor in range(1, 9):
        if amount % divisor == 0:
            chosen = divisor
    return chosen


def local_any(activations, pre_act, grad_act, kept_weight, block_cols):
    block = kept_weight.shape[-1]
    tok_count, width = activations.shape
    blocks_d = width // block
    dp_size = lax.axis_size("dp")
    grad_scale = 1.0 / math.sqrt(tok_count * dp_size)
    act_blocks = activations.reshape(tok_count, blocks_d, block)
    hidden_grad = hidden_gradient(pre_act, grad_act)
    grad_blocks = hidden_grad.reshape(tok_count, -1, block)
    col_ids = block_cols[0]
    kept_all = col_ids.shape[0]
    per_row = kept_all // blocks_d
    col_table = col_ids.reshape(blocks_d, per_row)
    row_group = group_of(blocks_d)
    group_count = blocks_d // row_group
    gathered = lax.all_gather(kept_weight, "dp", axis=1, tiled=True)
    whole_weights = gathered[0].reshape(blocks_d, per_row, block, block)

    def with_terms(group_index):
        first_row = group_index * row_group
        col_pick = lax.dynamic_slice_in_dim(col_table, first_row, row_group, 0).reshape(-1)
        grad_group = jnp.take(grad_blocks, col_pick, axis=1).reshape(
            tok_count, row_group, per_row, block
        )
        weight_group = lax.dynamic_slice_in_dim(whole_weights, first_row, row_group, 0)
        act_part = jnp.einsum(
            "trkf,rkdf->trd", grad_group, weight_group, preferred_element_type=jnp.float32
        )
        act_group = lax.dynamic_slice_in_dim(act_blocks, first_row, row_group, 1)
        block_term = (
            jnp.einsum("tra,trkf->rkaf", act_group, grad_group, preferred_element_type=jnp.float32)
            * grad_scale
        )
        return (act_part, block_term)

    act_parts, block_terms = lax.map(with_terms, jnp.arange(group_count, dtype=jnp.int32))
    summed = lax.psum_scatter(
        block_terms.reshape(kept_all, block, block), "dp", scatter_dimension=0, tiled=True
    )
    weight_grad = summed.astype(jnp.bfloat16).reshape(1, -1, block, block)
    partial_value = jnp.transpose(act_parts, (1, 0, 2, 3)).reshape(tok_count, width)
    act_grad = lax.psum(partial_value, "tensor").astype(jnp.bfloat16)
    return (weight_grad, act_grad)


SIDE, NEAR, FAR = 1, 2, 4
SETS = (0, SIDE, FAR, FAR | SIDE)
CHUNKS = (3, 5, 5, 3)


def columns_of(chunk_refs, spans):
    return jnp.concatenate(
        [jnp.concatenate([ref[:, span] for span in spans], axis=1) for ref in chunk_refs], axis=0
    )


def spans_of(cols_ref, first, count, block):
    return [
        pl.ds(pl.multiple_of(cols_ref[first + k] * block, block), block) for k in range(count)
    ]


def weight_term_kernel(
    per_row, rows, first_row, grad_scale, act_count, hid_count, place_ref, cols_ref, *refs
):
    act_refs, hid_refs = refs[:act_count], refs[act_count : act_count + hid_count]
    acc_refs, out_ref = refs[act_count + hid_count : -1], refs[-1]
    step_rows = out_ref.shape[0] // per_row
    block = out_ref.shape[1]
    group = 4 if per_row % 4 == 0 else 1

    @pl.loop(0, step_rows)
    def _(step_row):
        row = first_row + pl.program_id(0) * step_rows + step_row
        first = (place_ref[0] * rows + row) * per_row
        lanes = pl.ds(pl.multiple_of(row * block, block), block)
        act_t = jnp.concatenate([ref[:, lanes] for ref in act_refs], axis=0).T
        for part in range(per_row // group):
            start = part * group
            hid = columns_of(hid_refs, spans_of(cols_ref, first + start, group, block))
            term = (
                lax.dot_general(
                    act_t, hid, (((1,), (0,)), ((), ())), preferred_element_type=jnp.float32
                )
                * grad_scale
            )
            for k in range(group):
                value = term[:, k * block : (k + 1) * block]
                at = step_row * per_row + start + k
                for acc_ref in acc_refs:
                    value = value + acc_ref[at]
                out_ref[at] = value.astype(out_ref.dtype)


def weight_terms(
    place, cols, acts, hids, acc, first_row, count, rows, per_row, block, grad_scale, kind
):
    tok = acts[0][0].shape[0]
    step_rows = next(k for k in (3, 2, 1) if count % k == 0)

    def act_spec(which):
        def at(s, place_ref, _):
            return (0, {"unit": place_ref[0], "near": place_ref[1]}.get(which, which))

        return pl.BlockSpec((tok, rows * block), at)

    chunks = [chunk for hid in hids for chunk in hid]
    accs = [] if acc is None else [acc]
    unit_spec = pl.BlockSpec((step_rows * per_row, block, block), lambda s, *_: (s, 0, 0))
    acc_spec = pl.BlockSpec(
        (step_rows * per_row, block, block), lambda s, *_: (first_row // step_rows + s, 0, 0)
    )
    kept = count * per_row
    return pl.pallas_call(
        functools.partial(
            weight_term_kernel, per_row, rows, first_row, grad_scale, len(acts), len(chunks)
        ),
        out_shape=jax.ShapeDtypeStruct((kept, block, block), kind),
        grid_spec=pltpu.PrefetchScalarGridSpec(
            num_scalar_prefetch=2,
            grid=(count // step_rows,),
            in_specs=[act_spec(entry[1]) for entry in acts]
            + [pl.BlockSpec(chunk.shape, lambda s, *_: (0, 0)) for chunk in chunks]
            + [acc_spec] * len(accs),
            out_specs=unit_spec,
        ),
        cost_estimate=pl.CostEstimate(
            flops=2 * kept * len(hids) * tok * block * block,
            bytes_accessed=2 * len(hids) * tok * chunks[0].shape[1] + 8 * kept * block * block,
            transcendentals=0,
        ),
        name="weight_terms",
    )(place, cols, *[entry[0] for entry in acts], *chunks, *accs)


def act_kernel(per_row, rows, set_count, hid_count, place_ref, cols_ref, *refs):
    hid_refs = refs[:hid_count]
    sources = refs[hid_count : hid_count + 2]
    outs = refs[hid_count + 2 : -2]
    held, sems = refs[-2:]
    unit = pl.program_id(0)
    block = held.shape[-1]
    near = jnp.where(unit == 0, place_ref[2], 1 - place_ref[2])

    def copy_of(source, into):
        return pltpu.make_async_copy(source, held.at[into], sems.at[into])

    @pl.when(unit == 0)
    def _():
        for index, source in enumerate(sources):
            @pl.when(place_ref[2] == place_ref[1])
            def _():
                copy_of(source, index).start()

            @pl.when(place_ref[2] != place_ref[1])
            def _():
                copy_of(source, 1 - index).start()

    copy_of(sources[0], unit).wait()

    @pl.loop(0, rows)
    def _(row):
        first = ((place_ref[0] + NEAR * near) * rows + row) * per_row
        hid = columns_of(hid_refs, spans_of(cols_ref, first, per_row, block))
        weight = jnp.concatenate([held[unit, row * per_row + k] for k in range(per_row)], axis=1)
        part = lax.dot_general(
            hid, weight, (((1,), (1,)), ((), ())), preferred_element_type=jnp.float32
        ).astype(jnp.bfloat16)
        tok = part.shape[0] // set_count
        lanes = pl.ds(pl.multiple_of(row * block, block), block)

        @pl.when(unit == 0)
        def _():
            for k in range(set_count):
                outs[2 * k][:, lanes] = part[k * tok : (k + 1) * tok]

        @pl.when(unit == 1)
        def _():
            for k in range(set_count):
                outs[2 * k + 1][:, lanes] = part[k * tok : (k + 1) * tok]


def act_partials(place, cols, hids, weights, rows, per_row):
    block = weights[0].shape[-1]
    chunks = [chunk for hid in hids for chunk in hid]
    tok = sum(chunk.shape[0] for chunk in hids[0])
    out = pl.BlockSpec((tok, rows * block), lambda s, *_: (0, 0))
    shape = jax.ShapeDtypeStruct((tok, rows * block), jnp.bfloat16)
    kept = 2 * rows * per_row
    return pl.pallas_call(
        functools.partial(act_kernel, per_row, rows, len(hids), len(chunks)),
        out_shape=(shape,) * (2 * len(hids)),
        grid_spec=pltpu.PrefetchScalarGridSpec(
            num_scalar_prefetch=2,
            grid=(2,),
            in_specs=[pl.BlockSpec(chunk.shape, lambda s, *_: (0, 0)) for chunk in chunks]
            + [pl.BlockSpec(memory_space=pl.ANY)] * 2,
            out_specs=[out] * (2 * len(hids)),
            scratch_shapes=[
                pltpu.VMEM((2, rows * per_row, block, block), jnp.bfloat16),
                pltpu.SemaphoreType.DMA((2,)),
            ],
        ),
        cost_estimate=pl.CostEstimate(
            flops=2 * kept * len(hids) * tok * block * block,
            bytes_accessed=2 * len(hids) * tok * chunks[0].shape[1] + 2 * kept * block * block,
            transcendentals=0,
        ),
        name="act_partials",
    )(place, cols, *chunks, *weights)


def put_kernel(count, place_ref, *refs):
    ins, out_ref, sems = refs[:count], refs[-2], refs[-1]
    copies = []
    for index, ref in enumerate(ins):
        tok, span = ref.shape
        into = out_ref.at[
            pl.ds(pl.multiple_of(place_ref[count + index] * tok, tok), tok),
            pl.ds(pl.multiple_of(place_ref[index] * span, span), span),
        ]
        copies.append(pltpu.make_async_copy(ref, into, sems.at[index]))
        copies[-1].start()
    for copy in copies:
        copy.wait()


def put_units(units, parts, arrays, whole, shape):
    given = [] if whole is None else [whole]
    count = len(arrays)
    return pl.pallas_call(
        functools.partial(put_kernel, count),
        out_shape=jax.ShapeDtypeStruct(shape, jnp.bfloat16),
        grid_spec=pltpu.PrefetchScalarGridSpec(
            num_scalar_prefetch=1,
            grid=(1,),
            in_specs=[pl.BlockSpec(array.shape, lambda s, *_: (0, 0)) for array in arrays]
            + [pl.BlockSpec(memory_space=pl.ANY)] * len(given),
            out_specs=pl.BlockSpec(memory_space=pl.ANY),
            scratch_shapes=[pltpu.SemaphoreType.DMA((count,))],
        ),
        input_output_aliases={count + 1: 0} if given else {},
        cost_estimate=pl.CostEstimate(
            flops=0, bytes_accessed=4 * count * arrays[0].size, transcendentals=0
        ),
        name="put_units",
    )(jnp.stack(units + parts).astype(jnp.int32), *arrays, *given)


def add_kernel(sum_ref, part_ref, *refs):
    refs[-1][...] = (sum_ref[...] + part_ref[...].astype(jnp.float32)).astype(jnp.bfloat16)


def add_part(total, part, index, size, whole):
    steps = part.shape[0] // size
    given = [] if whole is None else [whole]
    shape = (size, *total.shape[1:])
    at = pl.BlockSpec(shape, lambda s: (index * steps + s, 0, 0))
    return pl.pallas_call(
        add_kernel,
        out_shape=jax.ShapeDtypeStruct(total.shape, jnp.bfloat16),
        grid=(steps,),
        in_specs=[at, pl.BlockSpec(shape, lambda s: (s, 0, 0))]
        + [pl.BlockSpec(memory_space=pl.ANY)] * len(given),
        out_specs=at,
        input_output_aliases={2: 0} if given else {},
        cost_estimate=pl.CostEstimate(
            flops=part.size, bytes_accessed=8 * part.size, transcendentals=0
        ),
        name="add_part",
    )(total, part, *given)


def add_up(left, right):
    return (left.astype(jnp.float32) + right.astype(jnp.float32)).astype(jnp.bfloat16)


def after(value, *others):
    return lax.optimization_barrier((value, *others))[0]


def local_bits(*arrays):
    return local_bits_body(*arrays)


def local_bits_body(activations, pre_act, grad_act, kept_weight, block_cols):
    block = kept_weight.shape[-1]
    tok, width = activations.shape
    dp_size, tensor_size = lax.axis_size("dp"), lax.axis_size("tensor")
    kept = kept_weight.shape[1]
    cols = block_cols[0]
    per_row = cols.shape[0] // (width // block)
    rows = kept // per_row
    span = rows * block
    grad_scale = 1.0 / math.sqrt(tok * dp_size)
    place = lax.axis_index("dp")
    near = (place // NEAR) % 2
    t_place = lax.axis_index("tensor")
    core = t_place % 2

    def swap(value, bits):
        return lax.ppermute(value, "dp", [(d, d ^ bits) for d in range(dp_size)])

    def partner(value, bit):
        return lax.ppermute(value, "tensor", [(t, t ^ bit) for t in range(tensor_size)])

    share = tok // tensor_size

    def share_of(unit, bits, *others):
        whole = after(activations, *others)
        part = lax.dynamic_slice(whole, (t_place * share, unit * span), (share, span))
        return swap(part, bits)

    def gathered(parts, *others):
        pieces = {0: jnp.concatenate([after(part, *others) for part in parts], axis=1)}
        bit = tensor_size // 2
        while bit:
            held = sorted(pieces)
            joined = jnp.concatenate([pieces[k] for k in held], axis=0)
            got = partner(joined, bit)
            for index, k in enumerate(held):
                pieces[k ^ bit] = got[index * share : (index + 1) * share]
            bit //= 2
        whole = jnp.zeros((tok, pieces[0].shape[1]), activations.dtype)
        for k, value in pieces.items():
            whole = lax.dynamic_update_slice_in_dim(whole, value, (t_place ^ k) * share, 0)
        return whole

    hid_own, hid_side, hid_far = [], [], []
    cut = 0
    for index, part in enumerate(CHUNKS):
        rows_of = slice(cut, cut + part * tok // sum(CHUNKS))
        cut = rows_of.stop
        pre_part = after(pre_act[rows_of], *hid_own[-1:])
        hid_own.append(hidden_gradient(pre_part, grad_act[rows_of]))
        if index < 2:
            hid_far.append(swap(hid_own[index], FAR))
        hid_side.append(swap(hid_own[-1], SIDE))

    side_share = lax.dynamic_slice_in_dim(activations, t_place * share, share, 0)
    options = [
        jnp.concatenate(
            [side_share[:, (base + NEAR * j) * span : (base + NEAR * j + 1) * span] for j in (0, 1)],
            axis=1,
        )
        for base in SETS
    ]
    wanted = (place ^ SIDE) & (FAR | SIDE)
    chosen = options[0]
    for base, option in zip(SETS[1:], options[1:]):
        chosen = jnp.where(wanted == base, option, chosen)
    side_acts = gathered([swap(after(chosen, hid_own[0]), SIDE)])
    near_shares = [
        share_of(place ^ NEAR ^ FAR, FAR, hid_own[1]),
        share_of(place ^ NEAR ^ FAR ^ SIDE, FAR | SIDE, hid_own[1]),
    ]
    own_weight = kept_weight[0]
    near_weight = swap(after(own_weight, hid_own[-1]), NEAR)

    near_place = jnp.stack([place ^ NEAR, 1 - near]).astype(jnp.int32)
    own_place = jnp.stack([place, near]).astype(jnp.int32)
    act_place = jnp.stack([place & (FAR | SIDE), near, core]).astype(jnp.int32)
    terms = functools.partial(
        weight_terms, cols=cols, rows=rows, per_row=per_row, block=block, grad_scale=grad_scale
    )
    first_terms = functools.partial(
        terms,
        acts=[(activations, "unit"), (side_acts, "near")],
        hids=[hid_own, hid_side],
        acc=None,
        first_row=0,
        count=rows,
        kind=jnp.float32,
    )
    weights = (own_weight, near_weight)

    def acts_of(hids, *others):
        return act_partials(after(act_place, *others), cols, hids, weights, rows, per_row)

    def core_sum(keep, give):
        return add_up(keep, partner(give, 1))

    def rest_sum(half, first_bit):
        bit = first_bit
        while bit < tensor_size:
            half = add_up(half, partner(half, bit))
            bit *= 2
        return half

    turn = (t_place // 2) % 2
    token_half = tok // 2

    def quarter_sum(half):
        keep = lax.dynamic_slice_in_dim(half, turn * token_half, token_half, 0)
        give = lax.dynamic_slice_in_dim(half, (1 - turn) * token_half, token_half, 0)
        return rest_sum(add_up(keep, partner(give, 2)), 4)

    hid_both = [swap(hid_far[0], SIDE)]
    hid_far.append(swap(after(hid_own[2], hid_far[0]), FAR))
    hid_both.append(swap(hid_far[1], SIDE))
    hid_far.append(swap(after(hid_own[3], hid_far[1]), FAR))
    near_sum = first_terms(after(near_place, hid_far[1]))
    own_sum = first_terms(after(own_place, near_sum))
    first_acts = acts_of([hid_own, hid_side], own_sum)
    near_acts = gathered(near_shares, first_acts[0])
    third = after(hid_far[2], first_acts[0])
    hid_both.append(swap(third, SIDE))
    own_shares = [
        share_of(place ^ FAR, FAR, third), share_of(place ^ FAR ^ SIDE, FAR | SIDE, third)
    ]
    halves = [rest_sum(core_sum(first_acts[2 * k], first_acts[2 * k + 1]), 2) for k in range(2)]
    fourth = after(hid_far[3], near_acts, *halves)
    hid_both.append(swap(fourth, SIDE))
    far_acts = acts_of([hid_far], fourth)
    far_core = core_sum(far_acts[0], far_acts[1])

    cuts = 2 if rows % 2 == 0 else 1
    came, last = [], far_core
    for k in range(cuts):
        last = terms(
            after(near_place, last),
            acts=[(near_acts, 0), (near_acts, 1)],
            hids=[hid_far, hid_both],
            acc=near_sum,
            first_row=k * (rows // cuts),
            count=rows // cuts,
            kind=jnp.bfloat16,
        )
        came.append(swap(last, NEAR))
    both_acts = acts_of([hid_both], last)
    both_core = core_sum(both_acts[0], both_acts[1])
    quarters = []
    for half, bits in ((far_core, FAR), (both_core, FAR | SIDE)):
        quarter = swap(quarter_sum(half), bits)
        quarters.append([quarter, partner(quarter, 2)])

    own_acts = gathered(own_shares, both_core)
    own_sum = terms(
        own_place,
        acts=[(own_acts, 0), (own_acts, 1)],
        hids=[hid_far, hid_both],
        acc=own_sum,
        first_row=0,
        count=rows,
        kind=jnp.float32,
    )
    weight_grad = None
    for k, value in enumerate(came):
        weight_grad = add_part(own_sum, value, k, per_row, weight_grad)

    unit = (place & (FAR | SIDE)) + NEAR * core
    mine = [halves[0], swap(halves[1], SIDE)]
    other = [partner(half, 1) for half in mine]
    units = [unit, unit ^ SIDE]
    act_grad = put_units(
        units + [u ^ NEAR for u in units], [core * 0] * 4, mine + other, None, activations.shape
    )
    for bits, pair in zip((FAR, FAR | SIDE), quarters):
        there = unit ^ bits
        act_grad = put_units(
            [there, there, there ^ NEAR, there ^ NEAR],
            [turn, 1 - turn] * 2,
            pair + [partner(value, 1) for value in pair],
            act_grad,
            activations.shape,
        )
    return (weight_grad[None], act_grad)


def fits_bits(mesh, activations, kept_weight):
    dp_size, tensor_size = mesh.shape["dp"], mesh.shape["tensor"]
    block = kept_weight.shape[-1]
    kept_all = kept_weight.shape[1]
    per_row = kept_all // (activations.shape[1] // block)
    return (
        dp_size == 2 * FAR
        and tensor_size >= 4
        and tensor_size & (tensor_size - 1) == 0
        and kept_all % (dp_size * per_row) == 0
        and activations.shape[0] % (dp_size * tensor_size * 16) == 0
        and activations.shape[0] % (dp_size * sum(CHUNKS) * 16) == 0
        and activations.shape[0] // dp_size <= 512
    )


def solution(mesh):
    def whole(activations, pre_act, grad_act, kept_weight, block_cols):
        fits = fits_bits(mesh, activations, kept_weight)
        return jax.shard_map(
            local_bits if fits else local_any,
            mesh=mesh,
            in_specs=(
                P("dp", None),
                P("dp", "tensor"),
                P("dp", "tensor"),
                P("tensor", "dp", None, None),
                P("tensor", None),
            ),
            out_specs=(P("tensor", "dp", None, None), P("dp", None)),
            check_vma=False,
        )(activations, pre_act, grad_act, kept_weight, block_cols)

    return whole
```

```python
import functools
import math

import jax
import jax.numpy as jnp
from jax import lax
from jax.experimental import pallas as pl
from jax.experimental.pallas import tpu as pltpu
from jax.sharding import PartitionSpec as P


gelu_coef = math.sqrt(2.0 / math.pi)


def gelu_slope(pre_vals):
    pre_wide = pre_vals.astype(jnp.float32)
    inner_arg = gelu_coef * (pre_wide + 0.044715 * pre_wide**3)
    tanh_val = jnp.tanh(inner_arg)
    return 0.5 * (1.0 + tanh_val) + 0.5 * pre_wide * (1.0 - tanh_val**2) * gelu_coef * (
        1.0 + 3.0 * 0.044715 * pre_wide**2
    )


def hidden_gradient(pre_act, grad_act):
    return (grad_act.astype(jnp.float32) * gelu_slope(pre_act)).astype(jnp.bfloat16)


def group_of(amount):
    chosen = 1
    for divisor in range(1, 9):
        if amount % divisor == 0:
            chosen = divisor
    return chosen


def local_any(activations, pre_act, grad_act, kept_weight, block_cols):
    block = kept_weight.shape[-1]
    tok_count, width = activations.shape
    blocks_d = width // block
    dp_size = lax.axis_size("dp")
    grad_scale = 1.0 / math.sqrt(tok_count * dp_size)
    act_blocks = activations.reshape(tok_count, blocks_d, block)
    hidden_grad = hidden_gradient(pre_act, grad_act)
    grad_blocks = hidden_grad.reshape(tok_count, -1, block)
    col_ids = block_cols[0]
    kept_all = col_ids.shape[0]
    per_row = kept_all // blocks_d
    col_table = col_ids.reshape(blocks_d, per_row)
    row_group = group_of(blocks_d)
    group_count = blocks_d // row_group
    gathered = lax.all_gather(kept_weight, "dp", axis=1, tiled=True)
    whole_weights = gathered[0].reshape(blocks_d, per_row, block, block)

    def with_terms(group_index):
        first_row = group_index * row_group
        col_pick = lax.dynamic_slice_in_dim(col_table, first_row, row_group, 0).reshape(-1)
        grad_group = jnp.take(grad_blocks, col_pick, axis=1).reshape(
            tok_count, row_group, per_row, block
        )
        weight_group = lax.dynamic_slice_in_dim(whole_weights, first_row, row_group, 0)
        act_part = jnp.einsum(
            "trkf,rkdf->trd", grad_group, weight_group, preferred_element_type=jnp.float32
        )
        act_group = lax.dynamic_slice_in_dim(act_blocks, first_row, row_group, 1)
        block_term = (
            jnp.einsum("tra,trkf->rkaf", act_group, grad_group, preferred_element_type=jnp.float32)
            * grad_scale
        )
        return (act_part, block_term)

    act_parts, block_terms = lax.map(with_terms, jnp.arange(group_count, dtype=jnp.int32))
    summed = lax.psum_scatter(
        block_terms.reshape(kept_all, block, block), "dp", scatter_dimension=0, tiled=True
    )
    weight_grad = summed.astype(jnp.bfloat16).reshape(1, -1, block, block)
    partial_value = jnp.transpose(act_parts, (1, 0, 2, 3)).reshape(tok_count, width)
    act_grad = lax.psum(partial_value, "tensor").astype(jnp.bfloat16)
    return (weight_grad, act_grad)


SIDE, NEAR, FAR = 1, 2, 4
CHUNKS = (3, 5, 5, 3)


def columns_of(chunk_refs, spans):
    return jnp.concatenate(
        [jnp.concatenate([ref[:, span] for span in spans], axis=1) for ref in chunk_refs], axis=0
    )


def spans_of(cols_ref, first, count, block):
    return [
        pl.ds(pl.multiple_of(cols_ref[first + k] * block, block), block) for k in range(count)
    ]


def weight_term_kernel(
    per_row, rows, first_row, grad_scale, act_count, hid_count, place_ref, cols_ref, *refs
):
    act_refs, hid_refs = refs[:act_count], refs[act_count : act_count + hid_count]
    acc_refs, out_ref = refs[act_count + hid_count : -1], refs[-1]
    step_rows = out_ref.shape[0] // per_row
    block = out_ref.shape[1]
    group = 4 if per_row % 4 == 0 else 1

    @pl.loop(0, step_rows)
    def _(step_row):
        row = first_row + pl.program_id(0) * step_rows + step_row
        first = (place_ref[0] * rows + row) * per_row
        lanes = pl.ds(pl.multiple_of(row * block, block), block)
        act_t = jnp.concatenate([ref[:, lanes] for ref in act_refs], axis=0).T
        for part in range(per_row // group):
            start = part * group
            hid = columns_of(hid_refs, spans_of(cols_ref, first + start, group, block))
            term = (
                lax.dot_general(
                    act_t, hid, (((1,), (0,)), ((), ())), preferred_element_type=jnp.float32
                )
                * grad_scale
            )
            for k in range(group):
                value = term[:, k * block : (k + 1) * block]
                at = step_row * per_row + start + k
                for acc_ref in acc_refs:
                    value = value + acc_ref[at]
                out_ref[at] = value.astype(out_ref.dtype)


def weight_terms(
    place, cols, acts, hids, acc, first_row, count, rows, per_row, block, grad_scale, kind
):
    tok = acts[0][0].shape[0]
    step_rows = next(k for k in (3, 2, 1) if count % k == 0)

    def at_of(place_ref):
        return {"unit": place_ref[0], "near": place_ref[1], "near_next": place_ref[1] + 2}

    def act_spec(which):
        def at(s, place_ref, _):
            return (0, at_of(place_ref)[which])

        return pl.BlockSpec((tok, rows * block), at)

    chunks = [chunk for hid in hids for chunk in hid]
    accs = [] if acc is None else [acc]
    unit_spec = pl.BlockSpec((step_rows * per_row, block, block), lambda s, *_: (s, 0, 0))
    acc_spec = pl.BlockSpec(
        (step_rows * per_row, block, block), lambda s, *_: (first_row // step_rows + s, 0, 0)
    )
    kept = count * per_row
    return pl.pallas_call(
        functools.partial(
            weight_term_kernel, per_row, rows, first_row, grad_scale, len(acts), len(chunks)
        ),
        out_shape=jax.ShapeDtypeStruct((kept, block, block), kind),
        grid_spec=pltpu.PrefetchScalarGridSpec(
            num_scalar_prefetch=2,
            grid=(count // step_rows,),
            in_specs=[act_spec(entry[1]) for entry in acts]
            + [pl.BlockSpec(chunk.shape, lambda s, *_: (0, 0)) for chunk in chunks]
            + [acc_spec] * len(accs),
            out_specs=unit_spec,
        ),
        cost_estimate=pl.CostEstimate(
            flops=2 * kept * len(hids) * tok * block * block,
            bytes_accessed=2 * len(hids) * tok * chunks[0].shape[1] + 8 * kept * block * block,
            transcendentals=0,
        ),
        name="weight_terms",
    )(place, cols, *[entry[0] for entry in acts], *chunks, *accs)


def act_kernel(per_row, rows, set_count, hid_count, place_ref, cols_ref, *refs):
    hid_refs = refs[:hid_count]
    sources = refs[hid_count : hid_count + 2]
    outs = refs[hid_count + 2 : -2]
    held, sems = refs[-2:]
    unit = pl.program_id(0)
    block = held.shape[-1]
    near = jnp.where(unit == 0, place_ref[2], 1 - place_ref[2])

    def copy_of(source, into):
        return pltpu.make_async_copy(source, held.at[into], sems.at[into])

    @pl.when(unit == 0)
    def _():
        for index, source in enumerate(sources):
            @pl.when(place_ref[2] == place_ref[1])
            def _():
                copy_of(source, index).start()

            @pl.when(place_ref[2] != place_ref[1])
            def _():
                copy_of(source, 1 - index).start()

    copy_of(sources[0], unit).wait()

    @pl.loop(0, rows)
    def _(row):
        first = ((place_ref[0] + NEAR * near) * rows + row) * per_row
        hid = columns_of(hid_refs, spans_of(cols_ref, first, per_row, block))
        weight = jnp.concatenate([held[unit, row * per_row + k] for k in range(per_row)], axis=1)
        part = lax.dot_general(
            hid, weight, (((1,), (1,)), ((), ())), preferred_element_type=jnp.float32
        ).astype(jnp.bfloat16)
        tok = part.shape[0] // set_count
        lanes = pl.ds(pl.multiple_of(row * block, block), block)

        @pl.when(unit == 0)
        def _():
            for k in range(set_count):
                outs[2 * k][:, lanes] = part[k * tok : (k + 1) * tok]

        @pl.when(unit == 1)
        def _():
            for k in range(set_count):
                outs[2 * k + 1][:, lanes] = part[k * tok : (k + 1) * tok]


def act_partials(place, cols, hids, weights, rows, per_row):
    block = weights[0].shape[-1]
    chunks = [chunk for hid in hids for chunk in hid]
    tok = sum(chunk.shape[0] for chunk in hids[0])
    out = pl.BlockSpec((tok, rows * block), lambda s, *_: (0, 0))
    shape = jax.ShapeDtypeStruct((tok, rows * block), jnp.bfloat16)
    kept = 2 * rows * per_row
    return pl.pallas_call(
        functools.partial(act_kernel, per_row, rows, len(hids), len(chunks)),
        out_shape=(shape,) * (2 * len(hids)),
        grid_spec=pltpu.PrefetchScalarGridSpec(
            num_scalar_prefetch=2,
            grid=(2,),
            in_specs=[pl.BlockSpec(chunk.shape, lambda s, *_: (0, 0)) for chunk in chunks]
            + [pl.BlockSpec(memory_space=pl.ANY)] * 2,
            out_specs=[out] * (2 * len(hids)),
            scratch_shapes=[
                pltpu.VMEM((2, rows * per_row, block, block), jnp.bfloat16),
                pltpu.SemaphoreType.DMA((2,)),
            ],
        ),
        cost_estimate=pl.CostEstimate(
            flops=2 * kept * len(hids) * tok * block * block,
            bytes_accessed=2 * len(hids) * tok * chunks[0].shape[1] + 2 * kept * block * block,
            transcendentals=0,
        ),
        name="act_partials",
    )(place, cols, *chunks, *weights)


def put_kernel(count, place_ref, *refs):
    ins, out_ref, sems = refs[:count], refs[-2], refs[-1]
    copies = []
    for index, ref in enumerate(ins):
        tok, span = ref.shape
        into = out_ref.at[
            pl.ds(pl.multiple_of(place_ref[count + index] * tok, tok), tok),
            pl.ds(pl.multiple_of(place_ref[index] * span, span), span),
        ]
        copies.append(pltpu.make_async_copy(ref, into, sems.at[index]))
        copies[-1].start()
    for copy in copies:
        copy.wait()


def put_units(units, parts, arrays, whole, shape):
    given = [] if whole is None else [whole]
    count = len(arrays)
    return pl.pallas_call(
        functools.partial(put_kernel, count),
        out_shape=jax.ShapeDtypeStruct(shape, jnp.bfloat16),
        grid_spec=pltpu.PrefetchScalarGridSpec(
            num_scalar_prefetch=1,
            grid=(1,),
            in_specs=[pl.BlockSpec(array.shape, lambda s, *_: (0, 0)) for array in arrays]
            + [pl.BlockSpec(memory_space=pl.ANY)] * len(given),
            out_specs=pl.BlockSpec(memory_space=pl.ANY),
            scratch_shapes=[pltpu.SemaphoreType.DMA((count,))],
        ),
        input_output_aliases={count + 1: 0} if given else {},
        cost_estimate=pl.CostEstimate(
            flops=0, bytes_accessed=4 * count * arrays[0].size, transcendentals=0
        ),
        name="put_units",
    )(jnp.stack(units + parts).astype(jnp.int32), *arrays, *given)


def add_kernel(sum_ref, part_ref, *refs):
    refs[-1][...] = (sum_ref[...] + part_ref[...].astype(jnp.float32)).astype(jnp.bfloat16)


def add_part(total, part, index, size, whole):
    steps = part.shape[0] // size
    given = [] if whole is None else [whole]
    shape = (size, *total.shape[1:])
    at = pl.BlockSpec(shape, lambda s: (index * steps + s, 0, 0))
    return pl.pallas_call(
        add_kernel,
        out_shape=jax.ShapeDtypeStruct(total.shape, jnp.bfloat16),
        grid=(steps,),
        in_specs=[at, pl.BlockSpec(shape, lambda s: (s, 0, 0))]
        + [pl.BlockSpec(memory_space=pl.ANY)] * len(given),
        out_specs=at,
        input_output_aliases={2: 0} if given else {},
        cost_estimate=pl.CostEstimate(
            flops=part.size, bytes_accessed=8 * part.size, transcendentals=0
        ),
        name="add_part",
    )(total, part, *given)


def add_up(left, right):
    return (left.astype(jnp.float32) + right.astype(jnp.float32)).astype(jnp.bfloat16)


def after(value, *others):
    return lax.optimization_barrier((value, *others))[0]


def local_bits(*arrays):
    return local_bits_body(*arrays)


def local_bits_body(activations, pre_act, grad_act, kept_weight, block_cols):
    block = kept_weight.shape[-1]
    tok, width = activations.shape
    dp_size, tensor_size = lax.axis_size("dp"), lax.axis_size("tensor")
    kept = kept_weight.shape[1]
    cols = block_cols[0]
    per_row = cols.shape[0] // (width // block)
    rows = kept // per_row
    span = rows * block
    grad_scale = 1.0 / math.sqrt(tok * dp_size)
    place = lax.axis_index("dp")
    near = (place // NEAR) % 2
    t_place = lax.axis_index("tensor")
    core = t_place % 2

    def swap(value, bits):
        return lax.ppermute(value, "dp", [(d, d ^ bits) for d in range(dp_size)])

    def partner(value, bit):
        return lax.ppermute(value, "tensor", [(t, t ^ bit) for t in range(tensor_size)])

    share = tok // tensor_size

    def share_of(bits, *others):
        mine = after(activations, *others)
        parts = [
            lax.dynamic_slice(
                mine,
                (t_place * share, (((place ^ bits) & (FAR | SIDE)) + NEAR * j) * span),
                (share, span),
            )
            for j in (0, 1)
        ]
        return swap(jnp.concatenate(parts, axis=1), bits)

    def gathered(parts, *others):
        pieces = {0: jnp.concatenate([after(part, *others) for part in parts], axis=1)}
        bit = tensor_size // 2
        while bit:
            held = sorted(pieces)
            joined = jnp.concatenate([pieces[k] for k in held], axis=0)
            got = partner(joined, bit)
            for index, k in enumerate(held):
                pieces[k ^ bit] = got[index * share : (index + 1) * share]
            bit //= 2
        whole = jnp.zeros((tok, pieces[0].shape[1]), activations.dtype)
        for k, value in pieces.items():
            whole = lax.dynamic_update_slice_in_dim(whole, value, (t_place ^ k) * share, 0)
        return whole

    hid_own, hid_side, hid_far = [], [], []
    cut = 0
    for index, part in enumerate(CHUNKS):
        rows_of = slice(cut, cut + part * tok // sum(CHUNKS))
        cut = rows_of.stop
        if hid_own:
            pre_act = after(pre_act, hid_own[-1])
        hid_own.append(hidden_gradient(pre_act[rows_of], grad_act[rows_of]))
        if index < 2:
            hid_far.append(swap(hid_own[index], FAR))
        hid_side.append(swap(hid_own[-1], SIDE))

    side_acts = gathered([share_of(SIDE, hid_own[1])])
    far_shares = [share_of(FAR, hid_own[1]), share_of(FAR | SIDE, hid_own[1])]
    own_weight = kept_weight[0]
    near_weight = swap(after(own_weight, hid_own[-1]), NEAR)

    near_place = jnp.stack([place ^ NEAR, 1 - near]).astype(jnp.int32)
    own_place = jnp.stack([place, near]).astype(jnp.int32)
    act_place = jnp.stack([place & (FAR | SIDE), near, core]).astype(jnp.int32)
    terms = functools.partial(
        weight_terms, cols=cols, rows=rows, per_row=per_row, block=block, grad_scale=grad_scale
    )
    first_terms = functools.partial(
        terms,
        acts=[(activations, "unit"), (side_acts, "near")],
        hids=[hid_own, hid_side],
        acc=None,
        first_row=0,
        count=rows,
        kind=jnp.float32,
    )
    weights = (own_weight, near_weight)

    def acts_of(hids, *others):
        return act_partials(after(act_place, *others), cols, hids, weights, rows, per_row)

    def core_sum(keep, give):
        return add_up(keep, partner(give, 1))

    def more_sum(value):
        bit = 4
        while bit < tensor_size:
            value = add_up(value, partner(value, bit))
            bit *= 2
        return value

    turn = (t_place // 2) % 2
    token_half = tok // 2

    def half_of(value, which):
        return lax.dynamic_slice_in_dim(value, which * token_half, token_half, 0)

    hid_both = [swap(hid_far[0], SIDE)]
    hid_far.append(swap(after(hid_own[2], hid_far[0]), FAR))
    hid_both.append(swap(hid_far[1], SIDE))
    hid_far.append(swap(after(hid_own[3], hid_far[1]), FAR))
    near_sum = first_terms(after(near_place, hid_far[1]))
    own_sum = first_terms(after(own_place, near_sum))
    far_acts = gathered(far_shares, own_sum)
    third = after(hid_far[2], own_sum)
    hid_both.append(swap(third, SIDE))
    parts = acts_of([hid_own, hid_side], third)
    near_cores = [core_sum(parts[0], parts[1]), core_sum(parts[2], parts[3])]
    near_got = [partner(value, 2) for value in near_cores]
    fourth = after(hid_far[3], far_acts, *near_cores)
    hid_both.append(swap(fourth, SIDE))
    parts = acts_of([hid_far], fourth)
    far_core = core_sum(parts[0], parts[1])
    far_got = partner(half_of(far_core, 1 - turn), 2)

    cuts = 2 if rows % 2 == 0 else 1
    came, last = [], far_core
    there = dict(hids=[hid_far, hid_both])
    for k in range(cuts):
        last = terms(
            after(near_place, last),
            acts=[(far_acts, "near"), (far_acts, "near_next")],
            acc=near_sum,
            first_row=k * (rows // cuts),
            count=rows // cuts,
            kind=jnp.bfloat16,
            **there,
        )
        came.append(swap(last, NEAR))
    far_sum = more_sum(add_up(after(half_of(far_core, turn), last), far_got))
    far_back = swap(far_sum, FAR)
    parts = acts_of([hid_both], far_sum)
    both_core = core_sum(parts[0], parts[1])
    both_got = partner(half_of(both_core, 1 - turn), 2)
    own_sum = terms(
        after(own_place, both_core),
        acts=[(far_acts, "near"), (far_acts, "near_next")],
        acc=own_sum,
        first_row=0,
        count=rows,
        kind=jnp.float32,
        **there,
    )
    both_sum = more_sum(add_up(after(half_of(both_core, turn), own_sum), both_got))
    both_back = swap(both_sum, FAR | SIDE)
    halves = [
        more_sum(add_up(after(value, both_sum), got)) for value, got in zip(near_cores, near_got)
    ]
    unit = (place & (FAR | SIDE)) + NEAR * core
    mine = [halves[0], swap(halves[1], SIDE)]
    quarters = []
    for value in (after(far_back, *halves), both_back):
        quarters.append([value, partner(value, 2)])

    def put(bits_of, arrays, parts_of, whole):
        there_units = [unit ^ bits for bits in bits_of]
        return put_units(
            there_units + [u ^ NEAR for u in there_units],
            parts_of * 2,
            arrays + [partner(value, 1) for value in arrays],
            whole,
            activations.shape,
        )

    zero = core * 0
    act_grad = put([0, SIDE], mine, [zero, zero], None)
    act_grad = put(
        [FAR, FAR, FAR | SIDE, FAR | SIDE], quarters[0] + quarters[1], [turn, 1 - turn] * 2, act_grad
    )
    weight_grad = None
    for k, value in enumerate(came):
        weight_grad = add_part(own_sum, value, k, per_row, weight_grad)
    return (weight_grad[None], act_grad)


def fits_bits(mesh, activations, kept_weight):
    dp_size, tensor_size = mesh.shape["dp"], mesh.shape["tensor"]
    block = kept_weight.shape[-1]
    kept_all = kept_weight.shape[1]
    per_row = kept_all // (activations.shape[1] // block)
    return (
        dp_size == 2 * FAR
        and tensor_size >= 4
        and tensor_size & (tensor_size - 1) == 0
        and kept_all % (dp_size * per_row) == 0
        and activations.shape[0] % (dp_size * tensor_size * 16) == 0
        and activations.shape[0] % (dp_size * sum(CHUNKS) * 16) == 0
        and activations.shape[0] // dp_size <= 512
    )


def solution(mesh):
    def whole(activations, pre_act, grad_act, kept_weight, block_cols):
        fits = fits_bits(mesh, activations, kept_weight)
        return jax.shard_map(
            local_bits if fits else local_any,
            mesh=mesh,
            in_specs=(
                P("dp", None),
                P("dp", "tensor"),
                P("dp", "tensor"),
                P("tensor", "dp", None, None),
                P("tensor", None),
            ),
            out_specs=(P("tensor", "dp", None, None), P("dp", None)),
            check_vma=False,
        )(activations, pre_act, grad_act, kept_weight, block_cols)

    return whole
```

```python
import functools
import math

import jax
import jax.numpy as jnp
from jax import lax
from jax.experimental import pallas as pl
from jax.experimental.pallas import tpu as pltpu
from jax.sharding import PartitionSpec as P


gelu_coef = math.sqrt(2.0 / math.pi)


def gelu_slope(pre_vals):
    pre_wide = pre_vals.astype(jnp.float32)
    inner_arg = gelu_coef * (pre_wide + 0.044715 * pre_wide**3)
    tanh_val = jnp.tanh(inner_arg)
    return 0.5 * (1.0 + tanh_val) + 0.5 * pre_wide * (1.0 - tanh_val**2) * gelu_coef * (
        1.0 + 3.0 * 0.044715 * pre_wide**2
    )


def hidden_gradient(pre_act, grad_act):
    return (grad_act.astype(jnp.float32) * gelu_slope(pre_act)).astype(jnp.bfloat16)


def group_of(amount):
    chosen = 1
    for divisor in range(1, 9):
        if amount % divisor == 0:
            chosen = divisor
    return chosen


def local_any(activations, pre_act, grad_act, kept_weight, block_cols):
    block = kept_weight.shape[-1]
    tok_count, width = activations.shape
    blocks_d = width // block
    dp_size = lax.axis_size("dp")
    grad_scale = 1.0 / math.sqrt(tok_count * dp_size)
    act_blocks = activations.reshape(tok_count, blocks_d, block)
    hidden_grad = hidden_gradient(pre_act, grad_act)
    grad_blocks = hidden_grad.reshape(tok_count, -1, block)
    col_ids = block_cols[0]
    kept_all = col_ids.shape[0]
    per_row = kept_all // blocks_d
    col_table = col_ids.reshape(blocks_d, per_row)
    row_group = group_of(blocks_d)
    group_count = blocks_d // row_group
    gathered = lax.all_gather(kept_weight, "dp", axis=1, tiled=True)
    whole_weights = gathered[0].reshape(blocks_d, per_row, block, block)

    def with_terms(group_index):
        first_row = group_index * row_group
        col_pick = lax.dynamic_slice_in_dim(col_table, first_row, row_group, 0).reshape(-1)
        grad_group = jnp.take(grad_blocks, col_pick, axis=1).reshape(
            tok_count, row_group, per_row, block
        )
        weight_group = lax.dynamic_slice_in_dim(whole_weights, first_row, row_group, 0)
        act_part = jnp.einsum(
            "trkf,rkdf->trd", grad_group, weight_group, preferred_element_type=jnp.float32
        )
        act_group = lax.dynamic_slice_in_dim(act_blocks, first_row, row_group, 1)
        block_term = (
            jnp.einsum("tra,trkf->rkaf", act_group, grad_group, preferred_element_type=jnp.float32)
            * grad_scale
        )
        return (act_part, block_term)

    act_parts, block_terms = lax.map(with_terms, jnp.arange(group_count, dtype=jnp.int32))
    summed = lax.psum_scatter(
        block_terms.reshape(kept_all, block, block), "dp", scatter_dimension=0, tiled=True
    )
    weight_grad = summed.astype(jnp.bfloat16).reshape(1, -1, block, block)
    partial_value = jnp.transpose(act_parts, (1, 0, 2, 3)).reshape(tok_count, width)
    act_grad = lax.psum(partial_value, "tensor").astype(jnp.bfloat16)
    return (weight_grad, act_grad)


SIDE, NEAR, FAR = 1, 2, 4
CHUNKS = (6, 5, 3, 2)


def columns_of(chunk_refs, spans):
    return jnp.concatenate(
        [jnp.concatenate([ref[:, span] for span in spans], axis=1) for ref in chunk_refs], axis=0
    )


def spans_of(cols_ref, first, count, block):
    return [
        pl.ds(pl.multiple_of(cols_ref[first + k] * block, block), block) for k in range(count)
    ]


def weight_term_kernel(
    per_row, rows, first_row, grad_scale, act_count, hid_count, place_ref, cols_ref, *refs
):
    act_refs, hid_refs = refs[:act_count], refs[act_count : act_count + hid_count]
    acc_refs, out_ref = refs[act_count + hid_count : -1], refs[-1]
    step_rows = out_ref.shape[0] // per_row
    block = out_ref.shape[1]
    group = 4 if per_row % 4 == 0 else 1

    @pl.loop(0, step_rows)
    def _(step_row):
        row = first_row + pl.program_id(0) * step_rows + step_row
        first = (place_ref[0] * rows + row) * per_row
        lanes = pl.ds(pl.multiple_of(row * block, block), block)
        act_t = jnp.concatenate([ref[:, lanes] for ref in act_refs], axis=0).T
        for part in range(per_row // group):
            start = part * group
            hid = columns_of(hid_refs, spans_of(cols_ref, first + start, group, block))
            term = (
                lax.dot_general(
                    act_t, hid, (((1,), (0,)), ((), ())), preferred_element_type=jnp.float32
                )
                * grad_scale
            )
            for k in range(group):
                value = term[:, k * block : (k + 1) * block]
                at = step_row * per_row + start + k
                for acc_ref in acc_refs:
                    value = value + acc_ref[at]
                out_ref[at] = value.astype(out_ref.dtype)


def weight_terms(
    place, cols, acts, hids, acc, first_row, count, rows, per_row, block, grad_scale, kind
):
    tok = acts[0][0].shape[0]
    step_rows = next(k for k in (3, 2, 1) if count % k == 0)

    def at_of(place_ref):
        return {"unit": place_ref[0], "near": place_ref[1], "near_next": place_ref[1] + 2}

    def act_spec(which):
        def at(s, place_ref, _):
            return (0, at_of(place_ref)[which])

        return pl.BlockSpec((tok, rows * block), at)

    chunks = [chunk for hid in hids for chunk in hid]
    accs = [] if acc is None else [acc]
    unit_spec = pl.BlockSpec((step_rows * per_row, block, block), lambda s, *_: (s, 0, 0))
    acc_spec = pl.BlockSpec(
        (step_rows * per_row, block, block), lambda s, *_: (first_row // step_rows + s, 0, 0)
    )
    kept = count * per_row
    return pl.pallas_call(
        functools.partial(
            weight_term_kernel, per_row, rows, first_row, grad_scale, len(acts), len(chunks)
        ),
        out_shape=jax.ShapeDtypeStruct((kept, block, block), kind),
        grid_spec=pltpu.PrefetchScalarGridSpec(
            num_scalar_prefetch=2,
            grid=(count // step_rows,),
            in_specs=[act_spec(entry[1]) for entry in acts]
            + [pl.BlockSpec(chunk.shape, lambda s, *_: (0, 0)) for chunk in chunks]
            + [acc_spec] * len(accs),
            out_specs=unit_spec,
        ),
        cost_estimate=pl.CostEstimate(
            flops=2 * kept * len(hids) * tok * block * block,
            bytes_accessed=2 * len(hids) * tok * chunks[0].shape[1] + 8 * kept * block * block,
            transcendentals=0,
        ),
        name="weight_terms",
    )(place, cols, *[entry[0] for entry in acts], *chunks, *accs)


def act_kernel(per_row, rows, set_count, hid_count, place_ref, cols_ref, *refs):
    hid_refs = refs[:hid_count]
    sources = refs[hid_count : hid_count + 2]
    outs = refs[hid_count + 2 : -2]
    held, sems = refs[-2:]
    unit = pl.program_id(0)
    block = held.shape[-1]
    near = jnp.where(unit == 0, place_ref[2], 1 - place_ref[2])

    def copy_of(source, into):
        return pltpu.make_async_copy(source, held.at[into], sems.at[into])

    @pl.when(unit == 0)
    def _():
        for index, source in enumerate(sources):
            @pl.when(place_ref[2] == place_ref[1])
            def _():
                copy_of(source, index).start()

            @pl.when(place_ref[2] != place_ref[1])
            def _():
                copy_of(source, 1 - index).start()

    copy_of(sources[0], unit).wait()

    @pl.loop(0, rows)
    def _(row):
        first = ((place_ref[0] + NEAR * near) * rows + row) * per_row
        hid = columns_of(hid_refs, spans_of(cols_ref, first, per_row, block))
        weight = jnp.concatenate([held[unit, row * per_row + k] for k in range(per_row)], axis=1)
        part = lax.dot_general(
            hid, weight, (((1,), (1,)), ((), ())), preferred_element_type=jnp.float32
        ).astype(jnp.bfloat16)
        tok = part.shape[0] // set_count
        lanes = pl.ds(pl.multiple_of(row * block, block), block)

        @pl.when(unit == 0)
        def _():
            for k in range(set_count):
                outs[2 * k][:, lanes] = part[k * tok : (k + 1) * tok]

        @pl.when(unit == 1)
        def _():
            for k in range(set_count):
                outs[2 * k + 1][:, lanes] = part[k * tok : (k + 1) * tok]


def act_partials(place, cols, hids, weights, rows, per_row):
    block = weights[0].shape[-1]
    chunks = [chunk for hid in hids for chunk in hid]
    tok = sum(chunk.shape[0] for chunk in hids[0])
    out = pl.BlockSpec((tok, rows * block), lambda s, *_: (0, 0))
    shape = jax.ShapeDtypeStruct((tok, rows * block), jnp.bfloat16)
    kept = 2 * rows * per_row
    return pl.pallas_call(
        functools.partial(act_kernel, per_row, rows, len(hids), len(chunks)),
        out_shape=(shape,) * (2 * len(hids)),
        grid_spec=pltpu.PrefetchScalarGridSpec(
            num_scalar_prefetch=2,
            grid=(2,),
            in_specs=[pl.BlockSpec(chunk.shape, lambda s, *_: (0, 0)) for chunk in chunks]
            + [pl.BlockSpec(memory_space=pl.ANY)] * 2,
            out_specs=[out] * (2 * len(hids)),
            scratch_shapes=[
                pltpu.VMEM((2, rows * per_row, block, block), jnp.bfloat16),
                pltpu.SemaphoreType.DMA((2,)),
            ],
        ),
        cost_estimate=pl.CostEstimate(
            flops=2 * kept * len(hids) * tok * block * block,
            bytes_accessed=2 * len(hids) * tok * chunks[0].shape[1] + 2 * kept * block * block,
            transcendentals=0,
        ),
        name="act_partials",
    )(place, cols, *chunks, *weights)


def put_kernel(count, place_ref, *refs):
    ins, out_ref, sems = refs[:count], refs[-2], refs[-1]
    copies = []
    for index, ref in enumerate(ins):
        tok, span = ref.shape
        into = out_ref.at[
            pl.ds(pl.multiple_of(place_ref[count + index] * tok, tok), tok),
            pl.ds(pl.multiple_of(place_ref[index] * span, span), span),
        ]
        copies.append(pltpu.make_async_copy(ref, into, sems.at[index]))
        copies[-1].start()
    for copy in copies:
        copy.wait()


def put_units(units, parts, arrays, whole, shape):
    given = [] if whole is None else [whole]
    count = len(arrays)
    return pl.pallas_call(
        functools.partial(put_kernel, count),
        out_shape=jax.ShapeDtypeStruct(shape, jnp.bfloat16),
        grid_spec=pltpu.PrefetchScalarGridSpec(
            num_scalar_prefetch=1,
            grid=(1,),
            in_specs=[pl.BlockSpec(array.shape, lambda s, *_: (0, 0)) for array in arrays]
            + [pl.BlockSpec(memory_space=pl.ANY)] * len(given),
            out_specs=pl.BlockSpec(memory_space=pl.ANY),
            scratch_shapes=[pltpu.SemaphoreType.DMA((count,))],
        ),
        input_output_aliases={count + 1: 0} if given else {},
        cost_estimate=pl.CostEstimate(
            flops=0, bytes_accessed=4 * count * arrays[0].size, transcendentals=0
        ),
        name="put_units",
    )(jnp.stack(units + parts).astype(jnp.int32), *arrays, *given)


def add_kernel(sum_ref, part_ref, *refs):
    refs[-1][...] = (sum_ref[...] + part_ref[...].astype(jnp.float32)).astype(jnp.bfloat16)


def add_part(total, part, index, size, whole):
    steps = part.shape[0] // size
    given = [] if whole is None else [whole]
    shape = (size, *total.shape[1:])
    at = pl.BlockSpec(shape, lambda s: (index * steps + s, 0, 0))
    return pl.pallas_call(
        add_kernel,
        out_shape=jax.ShapeDtypeStruct(total.shape, jnp.bfloat16),
        grid=(steps,),
        in_specs=[at, pl.BlockSpec(shape, lambda s: (s, 0, 0))]
        + [pl.BlockSpec(memory_space=pl.ANY)] * len(given),
        out_specs=at,
        input_output_aliases={2: 0} if given else {},
        cost_estimate=pl.CostEstimate(
            flops=part.size, bytes_accessed=8 * part.size, transcendentals=0
        ),
        name="add_part",
    )(total, part, *given)


def add_up(left, right):
    return (left.astype(jnp.float32) + right.astype(jnp.float32)).astype(jnp.bfloat16)


def after(value, *others):
    return lax.optimization_barrier((value, *others))[0]


def local_bits(*arrays):
    return local_bits_body(*arrays)


def local_bits_body(activations, pre_act, grad_act, kept_weight, block_cols):
    block = kept_weight.shape[-1]
    tok, width = activations.shape
    dp_size, tensor_size = lax.axis_size("dp"), lax.axis_size("tensor")
    kept = kept_weight.shape[1]
    cols = block_cols[0]
    per_row = cols.shape[0] // (width // block)
    rows = kept // per_row
    span = rows * block
    grad_scale = 1.0 / math.sqrt(tok * dp_size)
    place = lax.axis_index("dp")
    near = (place // NEAR) % 2
    t_place = lax.axis_index("tensor")
    core = t_place % 2

    def swap(value, bits):
        return lax.ppermute(value, "dp", [(d, d ^ bits) for d in range(dp_size)])

    def partner(value, bit):
        return lax.ppermute(value, "tensor", [(t, t ^ bit) for t in range(tensor_size)])

    share = tok // tensor_size

    def share_of(bits, *others):
        mine = after(activations, *others)
        parts = [
            lax.dynamic_slice(
                mine,
                (t_place * share, (((place ^ bits) & (FAR | SIDE)) + NEAR * j) * span),
                (share, span),
            )
            for j in (0, 1)
        ]
        return swap(jnp.concatenate(parts, axis=1), bits)

    def gathered(parts, *others):
        pieces = {0: jnp.concatenate([after(part, *others) for part in parts], axis=1)}
        bit = tensor_size // 2
        while bit:
            held = sorted(pieces)
            joined = jnp.concatenate([pieces[k] for k in held], axis=0)
            got = partner(joined, bit)
            for index, k in enumerate(held):
                pieces[k ^ bit] = got[index * share : (index + 1) * share]
            bit //= 2
        whole = jnp.zeros((tok, pieces[0].shape[1]), activations.dtype)
        for k, value in pieces.items():
            whole = lax.dynamic_update_slice_in_dim(whole, value, (t_place ^ k) * share, 0)
        return whole

    hid_own, hid_side, hid_far = [], [], []
    cut = 0
    for index, part in enumerate(CHUNKS):
        rows_of = slice(cut, cut + part * tok // sum(CHUNKS))
        cut = rows_of.stop
        if hid_own:
            pre_act = after(pre_act, hid_own[-1])
        hid_own.append(hidden_gradient(pre_act[rows_of], grad_act[rows_of]))
        if index == 0:
            hid_far.append(swap(hid_own[0], FAR))
        hid_side.append(swap(hid_own[-1], SIDE))

    side_acts = gathered([share_of(SIDE, hid_own[1])])
    far_shares = [share_of(FAR, hid_own[1]), share_of(FAR | SIDE, hid_own[1])]
    own_weight = kept_weight[0]
    near_weight = swap(after(own_weight, hid_own[0]), NEAR)

    near_place = jnp.stack([place ^ NEAR, 1 - near]).astype(jnp.int32)
    own_place = jnp.stack([place, near]).astype(jnp.int32)
    act_place = jnp.stack([place & (FAR | SIDE), near, core]).astype(jnp.int32)
    terms = functools.partial(
        weight_terms, cols=cols, rows=rows, per_row=per_row, block=block, grad_scale=grad_scale
    )
    first_terms = functools.partial(
        terms,
        acts=[(activations, "unit"), (side_acts, "near")],
        hids=[hid_own, hid_side],
        acc=None,
        first_row=0,
        count=rows,
        kind=jnp.float32,
    )
    weights = (own_weight, near_weight)

    def acts_of(hids, *others):
        return act_partials(after(act_place, *others), cols, hids, weights, rows, per_row)

    def core_sum(keep, give):
        return add_up(keep, partner(give, 1))

    def more_sum(value):
        bit = 4
        while bit < tensor_size:
            value = add_up(value, partner(value, bit))
            bit *= 2
        return value

    turn = (t_place // 2) % 2
    token_half = tok // 2

    def half_of(value, which):
        return lax.dynamic_slice_in_dim(value, which * token_half, token_half, 0)

    hid_both = [swap(hid_far[0], SIDE)]
    hid_far.append(swap(after(hid_own[1], hid_far[0]), FAR))
    near_sum = first_terms(after(near_place, hid_far[0]))
    own_sum = first_terms(after(own_place, near_sum))
    far_acts = gathered(far_shares, own_sum)
    second = after(hid_far[1], own_sum)
    hid_both.append(swap(second, SIDE))
    hid_far.append(swap(after(hid_own[2], second), FAR))
    parts = acts_of([hid_own, hid_side], second)
    third = after(hid_far[2], parts[0])
    hid_both.append(swap(third, SIDE))
    hid_far.append(swap(after(hid_own[3], third), FAR))
    near_cores = [core_sum(parts[0], parts[1]), core_sum(parts[2], parts[3])]
    near_got = [partner(value, 2) for value in near_cores]
    fourth = after(hid_far[3], far_acts, *near_cores)
    hid_both.append(swap(fourth, SIDE))
    parts = acts_of([hid_far], fourth)
    far_core = core_sum(parts[0], parts[1])
    far_got = partner(half_of(far_core, 1 - turn), 2)

    cuts = 2 if rows % 2 == 0 else 1
    came, last = [], far_core
    there = dict(hids=[hid_far, hid_both])
    for k in range(cuts):
        last = terms(
            after(near_place, last),
            acts=[(far_acts, "near"), (far_acts, "near_next")],
            acc=near_sum,
            first_row=k * (rows // cuts),
            count=rows // cuts,
            kind=jnp.bfloat16,
            **there,
        )
        came.append(swap(last, NEAR))
    far_sum = more_sum(add_up(after(half_of(far_core, turn), last), far_got))
    far_back = swap(far_sum, FAR)
    parts = acts_of([hid_both], far_sum)
    both_core = core_sum(parts[0], parts[1])
    both_got = partner(half_of(both_core, 1 - turn), 2)
    own_sum = terms(
        after(own_place, both_core),
        acts=[(far_acts, "near"), (far_acts, "near_next")],
        acc=own_sum,
        first_row=0,
        count=rows,
        kind=jnp.float32,
        **there,
    )
    both_sum = more_sum(add_up(after(half_of(both_core, turn), own_sum), both_got))
    both_back = swap(both_sum, FAR | SIDE)
    halves = [
        more_sum(add_up(after(value, both_sum), got)) for value, got in zip(near_cores, near_got)
    ]
    unit = (place & (FAR | SIDE)) + NEAR * core
    mine = [halves[0], swap(halves[1], SIDE)]

    def put(bits_of, arrays, parts_of, whole):
        there_units = [unit ^ bits for bits in bits_of]
        return put_units(
            there_units + [u ^ NEAR for u in there_units],
            parts_of * 2,
            arrays + [partner(value, 1) for value in arrays],
            whole,
            activations.shape,
        )

    weight_grad = add_part(own_sum, after(came[0], *halves), 0, per_row, None)
    far_back = after(far_back, weight_grad)
    far_pair = [far_back, partner(far_back, 2)]
    both_back = after(both_back, far_back)
    both_pair = [both_back, partner(both_back, 2)]
    zero = core * 0
    near_put = put([0, SIDE], mine, [zero, zero], None)
    for k, value in list(enumerate(came))[1:]:
        weight_grad = add_part(own_sum, after(value, near_put), k, per_row, weight_grad)
    act_grad = put(
        [FAR, FAR, FAR | SIDE, FAR | SIDE],
        far_pair + both_pair,
        [turn, 1 - turn] * 2,
        near_put,
    )
    return (weight_grad[None], act_grad)


def fits_bits(mesh, activations, kept_weight):
    dp_size, tensor_size = mesh.shape["dp"], mesh.shape["tensor"]
    block = kept_weight.shape[-1]
    kept_all = kept_weight.shape[1]
    per_row = kept_all // (activations.shape[1] // block)
    return (
        dp_size == 2 * FAR
        and tensor_size >= 4
        and tensor_size & (tensor_size - 1) == 0
        and kept_all % (dp_size * per_row) == 0
        and activations.shape[0] % (dp_size * tensor_size * 16) == 0
        and activations.shape[0] % (dp_size * sum(CHUNKS) * 16) == 0
        and activations.shape[0] // dp_size <= 512
    )


def solution(mesh):
    def whole(activations, pre_act, grad_act, kept_weight, block_cols):
        fits = fits_bits(mesh, activations, kept_weight)
        return jax.shard_map(
            local_bits if fits else local_any,
            mesh=mesh,
            in_specs=(
                P("dp", None),
                P("dp", "tensor"),
                P("dp", "tensor"),
                P("tensor", "dp", None, None),
                P("tensor", None),
            ),
            out_specs=(P("tensor", "dp", None, None), P("dp", None)),
            check_vma=False,
        )(activations, pre_act, grad_act, kept_weight, block_cols)

    return whole
```

```python
import functools
import math

import jax
import jax.numpy as jnp
from jax import lax
from jax.experimental import pallas as pl
from jax.experimental.pallas import tpu as pltpu
from jax.sharding import PartitionSpec as P


gelu_coef = math.sqrt(2.0 / math.pi)


def gelu_slope(pre_vals):
    pre_wide = pre_vals.astype(jnp.float32)
    inner_arg = gelu_coef * (pre_wide + 0.044715 * pre_wide**3)
    tanh_val = jnp.tanh(inner_arg)
    return 0.5 * (1.0 + tanh_val) + 0.5 * pre_wide * (1.0 - tanh_val**2) * gelu_coef * (
        1.0 + 3.0 * 0.044715 * pre_wide**2
    )


def hidden_gradient(pre_act, grad_act):
    return (grad_act.astype(jnp.float32) * gelu_slope(pre_act)).astype(jnp.bfloat16)


def group_of(amount):
    chosen = 1
    for divisor in range(1, 9):
        if amount % divisor == 0:
            chosen = divisor
    return chosen


def local_any(activations, pre_act, grad_act, kept_weight, block_cols):
    block = kept_weight.shape[-1]
    tok_count, width = activations.shape
    blocks_d = width // block
    dp_size = lax.axis_size("dp")
    grad_scale = 1.0 / math.sqrt(tok_count * dp_size)
    act_blocks = activations.reshape(tok_count, blocks_d, block)
    hidden_grad = hidden_gradient(pre_act, grad_act)
    grad_blocks = hidden_grad.reshape(tok_count, -1, block)
    col_ids = block_cols[0]
    kept_all = col_ids.shape[0]
    per_row = kept_all // blocks_d
    col_table = col_ids.reshape(blocks_d, per_row)
    row_group = group_of(blocks_d)
    group_count = blocks_d // row_group
    gathered = lax.all_gather(kept_weight, "dp", axis=1, tiled=True)
    whole_weights = gathered[0].reshape(blocks_d, per_row, block, block)

    def with_terms(group_index):
        first_row = group_index * row_group
        col_pick = lax.dynamic_slice_in_dim(col_table, first_row, row_group, 0).reshape(-1)
        grad_group = jnp.take(grad_blocks, col_pick, axis=1).reshape(
            tok_count, row_group, per_row, block
        )
        weight_group = lax.dynamic_slice_in_dim(whole_weights, first_row, row_group, 0)
        act_part = jnp.einsum(
            "trkf,rkdf->trd", grad_group, weight_group, preferred_element_type=jnp.float32
        )
        act_group = lax.dynamic_slice_in_dim(act_blocks, first_row, row_group, 1)
        block_term = (
            jnp.einsum("tra,trkf->rkaf", act_group, grad_group, preferred_element_type=jnp.float32)
            * grad_scale
        )
        return (act_part, block_term)

    act_parts, block_terms = lax.map(with_terms, jnp.arange(group_count, dtype=jnp.int32))
    summed = lax.psum_scatter(
        block_terms.reshape(kept_all, block, block), "dp", scatter_dimension=0, tiled=True
    )
    weight_grad = summed.astype(jnp.bfloat16).reshape(1, -1, block, block)
    partial_value = jnp.transpose(act_parts, (1, 0, 2, 3)).reshape(tok_count, width)
    act_grad = lax.psum(partial_value, "tensor").astype(jnp.bfloat16)
    return (weight_grad, act_grad)


SIDE, NEAR, FAR = 1, 2, 4
CHUNKS = (3, 5, 5, 3)


def columns_of(chunk_refs, spans):
    return jnp.concatenate(
        [jnp.concatenate([ref[:, span] for span in spans], axis=1) for ref in chunk_refs], axis=0
    )


def spans_of(cols_ref, first, count, block):
    return [
        pl.ds(pl.multiple_of(cols_ref[first + k] * block, block), block) for k in range(count)
    ]


def weight_term_kernel(
    per_row, rows, first_row, grad_scale, act_count, hid_count, place_ref, cols_ref, *refs
):
    act_refs, hid_refs = refs[:act_count], refs[act_count : act_count + hid_count]
    acc_refs, out_ref = refs[act_count + hid_count : -1], refs[-1]
    step_rows = out_ref.shape[0] // per_row
    block = out_ref.shape[1]
    group = 4 if per_row % 4 == 0 else 1

    @pl.loop(0, step_rows)
    def _(step_row):
        row = first_row + pl.program_id(0) * step_rows + step_row
        first = (place_ref[0] * rows + row) * per_row
        lanes = pl.ds(pl.multiple_of(row * block, block), block)
        act_t = jnp.concatenate([ref[:, lanes] for ref in act_refs], axis=0).T
        for part in range(per_row // group):
            start = part * group
            hid = columns_of(hid_refs, spans_of(cols_ref, first + start, group, block))
            term = (
                lax.dot_general(
                    act_t, hid, (((1,), (0,)), ((), ())), preferred_element_type=jnp.float32
                )
                * grad_scale
            )
            for k in range(group):
                value = term[:, k * block : (k + 1) * block]
                at = step_row * per_row + start + k
                for acc_ref in acc_refs:
                    value = value + acc_ref[at]
                out_ref[at] = value.astype(out_ref.dtype)


def weight_terms(
    place, cols, acts, hids, acc, first_row, count, rows, per_row, block, grad_scale, kind
):
    tok = acts[0][0].shape[0]
    step_rows = next(k for k in (3, 2, 1) if count % k == 0)

    def at_of(place_ref):
        return {"unit": place_ref[0], "near": place_ref[1], "near_next": place_ref[1] + 2}

    def act_spec(which):
        def at(s, place_ref, _):
            return (0, at_of(place_ref)[which])

        return pl.BlockSpec((tok, rows * block), at)

    chunks = [chunk for hid in hids for chunk in hid]
    accs = [] if acc is None else [acc]
    unit_spec = pl.BlockSpec((step_rows * per_row, block, block), lambda s, *_: (s, 0, 0))
    acc_spec = pl.BlockSpec(
        (step_rows * per_row, block, block), lambda s, *_: (first_row // step_rows + s, 0, 0)
    )
    kept = count * per_row
    return pl.pallas_call(
        functools.partial(
            weight_term_kernel, per_row, rows, first_row, grad_scale, len(acts), len(chunks)
        ),
        out_shape=jax.ShapeDtypeStruct((kept, block, block), kind),
        grid_spec=pltpu.PrefetchScalarGridSpec(
            num_scalar_prefetch=2,
            grid=(count // step_rows,),
            in_specs=[act_spec(entry[1]) for entry in acts]
            + [pl.BlockSpec(chunk.shape, lambda s, *_: (0, 0)) for chunk in chunks]
            + [acc_spec] * len(accs),
            out_specs=unit_spec,
        ),
        cost_estimate=pl.CostEstimate(
            flops=2 * kept * len(hids) * tok * block * block,
            bytes_accessed=2 * len(hids) * tok * chunks[0].shape[1] + 8 * kept * block * block,
            transcendentals=0,
        ),
        name="weight_terms",
    )(place, cols, *[entry[0] for entry in acts], *chunks, *accs)


def act_kernel(per_row, rows, set_count, hid_count, place_ref, cols_ref, *refs):
    hid_refs = refs[:hid_count]
    sources = refs[hid_count : hid_count + 2]
    outs = refs[hid_count + 2 : -2]
    held, sems = refs[-2:]
    unit = pl.program_id(0)
    block = held.shape[-1]
    near = jnp.where(unit == 0, place_ref[2], 1 - place_ref[2])

    def copy_of(source, into):
        return pltpu.make_async_copy(source, held.at[into], sems.at[into])

    @pl.when(unit == 0)
    def _():
        for index, source in enumerate(sources):
            @pl.when(place_ref[2] == place_ref[1])
            def _():
                copy_of(source, index).start()

            @pl.when(place_ref[2] != place_ref[1])
            def _():
                copy_of(source, 1 - index).start()

    copy_of(sources[0], unit).wait()

    @pl.loop(0, rows)
    def _(row):
        first = ((place_ref[0] + NEAR * near) * rows + row) * per_row
        hid = columns_of(hid_refs, spans_of(cols_ref, first, per_row, block))
        weight = jnp.concatenate([held[unit, row * per_row + k] for k in range(per_row)], axis=1)
        part = lax.dot_general(
            hid, weight, (((1,), (1,)), ((), ())), preferred_element_type=jnp.float32
        ).astype(jnp.bfloat16)
        tok = part.shape[0] // set_count
        lanes = pl.ds(pl.multiple_of(row * block, block), block)

        @pl.when(unit == 0)
        def _():
            for k in range(set_count):
                outs[2 * k][:, lanes] = part[k * tok : (k + 1) * tok]

        @pl.when(unit == 1)
        def _():
            for k in range(set_count):
                outs[2 * k + 1][:, lanes] = part[k * tok : (k + 1) * tok]


def act_partials(place, cols, hids, weights, rows, per_row):
    block = weights[0].shape[-1]
    chunks = [chunk for hid in hids for chunk in hid]
    tok = sum(chunk.shape[0] for chunk in hids[0])
    out = pl.BlockSpec((tok, rows * block), lambda s, *_: (0, 0))
    shape = jax.ShapeDtypeStruct((tok, rows * block), jnp.bfloat16)
    kept = 2 * rows * per_row
    return pl.pallas_call(
        functools.partial(act_kernel, per_row, rows, len(hids), len(chunks)),
        out_shape=(shape,) * (2 * len(hids)),
        grid_spec=pltpu.PrefetchScalarGridSpec(
            num_scalar_prefetch=2,
            grid=(2,),
            in_specs=[pl.BlockSpec(chunk.shape, lambda s, *_: (0, 0)) for chunk in chunks]
            + [pl.BlockSpec(memory_space=pl.ANY)] * 2,
            out_specs=[out] * (2 * len(hids)),
            scratch_shapes=[
                pltpu.VMEM((2, rows * per_row, block, block), jnp.bfloat16),
                pltpu.SemaphoreType.DMA((2,)),
            ],
        ),
        cost_estimate=pl.CostEstimate(
            flops=2 * kept * len(hids) * tok * block * block,
            bytes_accessed=2 * len(hids) * tok * chunks[0].shape[1] + 2 * kept * block * block,
            transcendentals=0,
        ),
        name="act_partials",
    )(place, cols, *chunks, *weights)


def put_kernel(count, place_ref, *refs):
    ins, out_ref, sems = refs[:count], refs[-2], refs[-1]
    copies = []
    for index, ref in enumerate(ins):
        tok, span = ref.shape
        into = out_ref.at[
            pl.ds(pl.multiple_of(place_ref[count + index] * tok, tok), tok),
            pl.ds(pl.multiple_of(place_ref[index] * span, span), span),
        ]
        copies.append(pltpu.make_async_copy(ref, into, sems.at[index]))
        copies[-1].start()
    for copy in copies:
        copy.wait()


def put_units(units, parts, arrays, whole, shape):
    given = [] if whole is None else [whole]
    count = len(arrays)
    return pl.pallas_call(
        functools.partial(put_kernel, count),
        out_shape=jax.ShapeDtypeStruct(shape, jnp.bfloat16),
        grid_spec=pltpu.PrefetchScalarGridSpec(
            num_scalar_prefetch=1,
            grid=(1,),
            in_specs=[pl.BlockSpec(array.shape, lambda s, *_: (0, 0)) for array in arrays]
            + [pl.BlockSpec(memory_space=pl.ANY)] * len(given),
            out_specs=pl.BlockSpec(memory_space=pl.ANY),
            scratch_shapes=[pltpu.SemaphoreType.DMA((count,))],
        ),
        input_output_aliases={count + 1: 0} if given else {},
        cost_estimate=pl.CostEstimate(
            flops=0, bytes_accessed=4 * count * arrays[0].size, transcendentals=0
        ),
        name="put_units",
    )(jnp.stack(units + parts).astype(jnp.int32), *arrays, *given)


def add_kernel(sum_ref, part_ref, *refs):
    refs[-1][...] = (sum_ref[...] + part_ref[...].astype(jnp.float32)).astype(jnp.bfloat16)


def add_part(total, part, index, size, whole):
    steps = part.shape[0] // size
    given = [] if whole is None else [whole]
    shape = (size, *total.shape[1:])
    at = pl.BlockSpec(shape, lambda s: (index * steps + s, 0, 0))
    return pl.pallas_call(
        add_kernel,
        out_shape=jax.ShapeDtypeStruct(total.shape, jnp.bfloat16),
        grid=(steps,),
        in_specs=[at, pl.BlockSpec(shape, lambda s: (s, 0, 0))]
        + [pl.BlockSpec(memory_space=pl.ANY)] * len(given),
        out_specs=at,
        input_output_aliases={2: 0} if given else {},
        cost_estimate=pl.CostEstimate(
            flops=part.size, bytes_accessed=8 * part.size, transcendentals=0
        ),
        name="add_part",
    )(total, part, *given)


def add_up(left, right):
    return (left.astype(jnp.float32) + right.astype(jnp.float32)).astype(jnp.bfloat16)


def after(value, *others):
    return lax.optimization_barrier((value, *others))[0]


def local_bits(*arrays):
    return local_bits_body(*arrays)


def local_bits_body(activations, pre_act, grad_act, kept_weight, block_cols):
    block = kept_weight.shape[-1]
    tok, width = activations.shape
    dp_size, tensor_size = lax.axis_size("dp"), lax.axis_size("tensor")
    kept = kept_weight.shape[1]
    cols = block_cols[0]
    per_row = cols.shape[0] // (width // block)
    rows = kept // per_row
    span = rows * block
    grad_scale = 1.0 / math.sqrt(tok * dp_size)
    place = lax.axis_index("dp")
    near = (place // NEAR) % 2
    t_place = lax.axis_index("tensor")
    core = t_place % 2

    def swap(value, bits):
        return lax.ppermute(value, "dp", [(d, d ^ bits) for d in range(dp_size)])

    def partner(value, bit):
        return lax.ppermute(value, "tensor", [(t, t ^ bit) for t in range(tensor_size)])

    share = tok // tensor_size

    def share_of(bits, *others):
        mine = after(activations, *others)
        parts = [
            lax.dynamic_slice(
                mine,
                (t_place * share, (((place ^ bits) & (FAR | SIDE)) + NEAR * j) * span),
                (share, span),
            )
            for j in (0, 1)
        ]
        return swap(jnp.concatenate(parts, axis=1), bits)

    def gathered(parts, *others):
        pieces = {0: jnp.concatenate([after(part, *others) for part in parts], axis=1)}
        bit = tensor_size // 2
        while bit:
            held = sorted(pieces)
            joined = jnp.concatenate([pieces[k] for k in held], axis=0)
            got = partner(joined, bit)
            for index, k in enumerate(held):
                pieces[k ^ bit] = got[index * share : (index + 1) * share]
            bit //= 2
        whole = jnp.zeros((tok, pieces[0].shape[1]), activations.dtype)
        for k, value in pieces.items():
            whole = lax.dynamic_update_slice_in_dim(whole, value, (t_place ^ k) * share, 0)
        return whole

    hid_own, hid_side, hid_far = [], [], []
    cut = 0
    for index, part in enumerate(CHUNKS):
        rows_of = slice(cut, cut + part * tok // sum(CHUNKS))
        cut = rows_of.stop
        if hid_own:
            pre_act = after(pre_act, hid_own[-1])
        hid_own.append(hidden_gradient(pre_act[rows_of], grad_act[rows_of]))
        if index < 2:
            hid_far.append(swap(hid_own[index], FAR))
        hid_side.append(swap(hid_own[-1], SIDE))

    side_acts = gathered([share_of(SIDE, hid_own[1])])
    far_shares = [share_of(FAR, hid_own[1]), share_of(FAR | SIDE, hid_own[1])]
    own_weight = kept_weight[0]
    near_weight = swap(after(own_weight, hid_own[-1]), NEAR)

    near_place = jnp.stack([place ^ NEAR, 1 - near]).astype(jnp.int32)
    own_place = jnp.stack([place, near]).astype(jnp.int32)
    act_place = jnp.stack([place & (FAR | SIDE), near, core]).astype(jnp.int32)
    terms = functools.partial(
        weight_terms, cols=cols, rows=rows, per_row=per_row, block=block, grad_scale=grad_scale
    )
    first_terms = functools.partial(
        terms,
        acts=[(activations, "unit"), (side_acts, "near")],
        hids=[hid_own, hid_side],
        acc=None,
        first_row=0,
        count=rows,
        kind=jnp.float32,
    )
    weights = (own_weight, near_weight)

    def acts_of(hids, *others):
        return act_partials(after(act_place, *others), cols, hids, weights, rows, per_row)

    def core_sum(keep, give):
        return add_up(keep, partner(give, 1))

    def more_sum(value):
        bit = 4
        while bit < tensor_size:
            value = add_up(value, partner(value, bit))
            bit *= 2
        return value

    turn = (t_place // 2) % 2
    token_half = tok // 2

    def half_of(value, which):
        return lax.dynamic_slice_in_dim(value, which * token_half, token_half, 0)

    hid_both = [swap(hid_far[0], SIDE)]
    hid_far.append(swap(after(hid_own[2], hid_far[0]), FAR))
    hid_both.append(swap(hid_far[1], SIDE))
    hid_far.append(swap(after(hid_own[3], hid_far[1]), FAR))
    near_sum = first_terms(after(near_place, hid_far[1]))
    own_sum = first_terms(after(own_place, near_sum))
    far_acts = gathered(far_shares, own_sum)
    third = after(hid_far[2], own_sum)
    hid_both.append(swap(third, SIDE))
    fourth = after(hid_far[3], third)
    hid_both.append(swap(fourth, SIDE))
    parts = acts_of([hid_own, hid_side], fourth)
    near_cores = [core_sum(parts[0], parts[1]), core_sum(parts[2], parts[3])]
    near_got = [partner(value, 2) for value in near_cores]
    parts = acts_of([hid_far], far_acts, *near_cores)
    far_core = core_sum(parts[0], parts[1])
    far_got = partner(half_of(far_core, 1 - turn), 2)

    cuts = 2 if rows % 2 == 0 else 1
    there = dict(
        acts=[(far_acts, "near"), (far_acts, "near_next")], hids=[hid_far, hid_both]
    )

    def near_part(k, *others):
        part = terms(
            after(near_place, *others),
            acc=near_sum,
            first_row=k * (rows // cuts),
            count=rows // cuts,
            kind=jnp.bfloat16,
            **there,
        )
        return part, swap(part, NEAR)

    last, got = near_part(0, far_core)
    came = [got]
    parts = acts_of([hid_both], last)
    both_core = core_sum(parts[0], parts[1])
    both_got = partner(half_of(both_core, 1 - turn), 2)
    far_sum = more_sum(add_up(after(half_of(far_core, turn), both_core), far_got))
    far_back = swap(far_sum, FAR)
    for k in range(1, cuts):
        last, got = near_part(k, far_sum)
        came.append(got)
    both_sum = more_sum(add_up(after(half_of(both_core, turn), last), both_got))
    both_back = swap(both_sum, FAR | SIDE)
    own_sum = terms(
        after(own_place, both_sum), acc=own_sum, first_row=0, count=rows, kind=jnp.float32, **there
    )
    halves = [
        more_sum(add_up(after(value, own_sum), got)) for value, got in zip(near_cores, near_got)
    ]
    unit = (place & (FAR | SIDE)) + NEAR * core
    mine = [halves[0], swap(halves[1], SIDE)]

    def put(bits_of, arrays, parts_of, whole):
        there_units = [unit ^ bits for bits in bits_of]
        return put_units(
            there_units + [u ^ NEAR for u in there_units],
            parts_of * 2,
            arrays + [partner(value, 1) for value in arrays],
            whole,
            activations.shape,
        )

    weight_grad = add_part(own_sum, after(came[0], *halves), 0, per_row, None)
    far_back = after(far_back, weight_grad)
    far_pair = [far_back, partner(far_back, 2)]
    both_back = after(both_back, far_back)
    both_pair = [both_back, partner(both_back, 2)]
    zero = core * 0
    near_put = put([0, SIDE], mine, [zero, zero], None)
    act_grad = put(
        [FAR, FAR, FAR | SIDE, FAR | SIDE],
        far_pair + both_pair,
        [turn, 1 - turn] * 2,
        near_put,
    )
    for k in range(1, cuts):
        weight_grad = add_part(own_sum, after(came[k], near_put), k, per_row, weight_grad)
    return (weight_grad[None], act_grad)


def fits_bits(mesh, activations, kept_weight):
    dp_size, tensor_size = mesh.shape["dp"], mesh.shape["tensor"]
    block = kept_weight.shape[-1]
    kept_all = kept_weight.shape[1]
    per_row = kept_all // (activations.shape[1] // block)
    return (
        dp_size == 2 * FAR
        and tensor_size >= 4
        and tensor_size & (tensor_size - 1) == 0
        and kept_all % (dp_size * per_row) == 0
        and activations.shape[0] % (dp_size * tensor_size * 16) == 0
        and activations.shape[0] % (dp_size * sum(CHUNKS) * 16) == 0
        and activations.shape[0] // dp_size <= 512
    )


def solution(mesh):
    def whole(activations, pre_act, grad_act, kept_weight, block_cols):
        fits = fits_bits(mesh, activations, kept_weight)
        return jax.shard_map(
            local_bits if fits else local_any,
            mesh=mesh,
            in_specs=(
                P("dp", None),
                P("dp", "tensor"),
                P("dp", "tensor"),
                P("tensor", "dp", None, None),
                P("tensor", None),
            ),
            out_specs=(P("tensor", "dp", None, None), P("dp", None)),
            check_vma=False,
        )(activations, pre_act, grad_act, kept_weight, block_cols)

    return whole
```

```python
import functools
import math

import jax
import jax.numpy as jnp
from jax import lax
from jax.experimental import pallas as pl
from jax.experimental.pallas import tpu as pltpu
from jax.sharding import PartitionSpec as P


gelu_coef = math.sqrt(2.0 / math.pi)


def gelu_slope(pre_vals):
    pre_wide = pre_vals.astype(jnp.float32)
    inner_arg = gelu_coef * (pre_wide + 0.044715 * pre_wide**3)
    tanh_val = jnp.tanh(inner_arg)
    return 0.5 * (1.0 + tanh_val) + 0.5 * pre_wide * (1.0 - tanh_val**2) * gelu_coef * (
        1.0 + 3.0 * 0.044715 * pre_wide**2
    )


def hidden_gradient(pre_act, grad_act):
    return (grad_act.astype(jnp.float32) * gelu_slope(pre_act)).astype(jnp.bfloat16)


def group_of(amount):
    chosen = 1
    for divisor in range(1, 9):
        if amount % divisor == 0:
            chosen = divisor
    return chosen


def local_any(activations, pre_act, grad_act, kept_weight, block_cols):
    block = kept_weight.shape[-1]
    tok_count, width = activations.shape
    blocks_d = width // block
    dp_size = lax.axis_size("dp")
    grad_scale = 1.0 / math.sqrt(tok_count * dp_size)
    act_blocks = activations.reshape(tok_count, blocks_d, block)
    hidden_grad = hidden_gradient(pre_act, grad_act)
    grad_blocks = hidden_grad.reshape(tok_count, -1, block)
    col_ids = block_cols[0]
    kept_all = col_ids.shape[0]
    per_row = kept_all // blocks_d
    col_table = col_ids.reshape(blocks_d, per_row)
    row_group = group_of(blocks_d)
    group_count = blocks_d // row_group
    gathered = lax.all_gather(kept_weight, "dp", axis=1, tiled=True)
    whole_weights = gathered[0].reshape(blocks_d, per_row, block, block)

    def with_terms(group_index):
        first_row = group_index * row_group
        col_pick = lax.dynamic_slice_in_dim(col_table, first_row, row_group, 0).reshape(-1)
        grad_group = jnp.take(grad_blocks, col_pick, axis=1).reshape(
            tok_count, row_group, per_row, block
        )
        weight_group = lax.dynamic_slice_in_dim(whole_weights, first_row, row_group, 0)
        act_part = jnp.einsum(
            "trkf,rkdf->trd", grad_group, weight_group, preferred_element_type=jnp.float32
        )
        act_group = lax.dynamic_slice_in_dim(act_blocks, first_row, row_group, 1)
        block_term = (
            jnp.einsum("tra,trkf->rkaf", act_group, grad_group, preferred_element_type=jnp.float32)
            * grad_scale
        )
        return (act_part, block_term)

    act_parts, block_terms = lax.map(with_terms, jnp.arange(group_count, dtype=jnp.int32))
    summed = lax.psum_scatter(
        block_terms.reshape(kept_all, block, block), "dp", scatter_dimension=0, tiled=True
    )
    weight_grad = summed.astype(jnp.bfloat16).reshape(1, -1, block, block)
    partial_value = jnp.transpose(act_parts, (1, 0, 2, 3)).reshape(tok_count, width)
    act_grad = lax.psum(partial_value, "tensor").astype(jnp.bfloat16)
    return (weight_grad, act_grad)


SIDE, NEAR, FAR = 1, 2, 4
CHUNKS = (3, 5, 5, 3)


def columns_of(chunk_refs, spans):
    return jnp.concatenate(
        [jnp.concatenate([ref[:, span] for span in spans], axis=1) for ref in chunk_refs], axis=0
    )


def spans_of(cols_ref, first, count, block):
    return [
        pl.ds(pl.multiple_of(cols_ref[first + k] * block, block), block) for k in range(count)
    ]


def weight_term_kernel(
    per_row, rows, first_row, grad_scale, act_count, hid_count, place_ref, cols_ref, *refs
):
    act_refs, hid_refs = refs[:act_count], refs[act_count : act_count + hid_count]
    acc_refs, out_ref = refs[act_count + hid_count : -1], refs[-1]
    step_rows = out_ref.shape[0] // per_row
    block = out_ref.shape[1]
    group = 4 if per_row % 4 == 0 else 1

    @pl.loop(0, step_rows)
    def _(step_row):
        row = first_row + pl.program_id(0) * step_rows + step_row
        first = (place_ref[0] * rows + row) * per_row
        lanes = pl.ds(pl.multiple_of(row * block, block), block)
        act_t = jnp.concatenate([ref[:, lanes] for ref in act_refs], axis=0).T
        for part in range(per_row // group):
            start = part * group
            hid = columns_of(hid_refs, spans_of(cols_ref, first + start, group, block))
            term = (
                lax.dot_general(
                    act_t, hid, (((1,), (0,)), ((), ())), preferred_element_type=jnp.float32
                )
                * grad_scale
            )
            for k in range(group):
                value = term[:, k * block : (k + 1) * block]
                at = step_row * per_row + start + k
                for acc_ref in acc_refs:
                    value = value + acc_ref[at]
                out_ref[at] = value.astype(out_ref.dtype)


def weight_terms(
    place, cols, acts, hids, acc, first_row, count, rows, per_row, block, grad_scale, kind
):
    tok = acts[0][0].shape[0]
    step_rows = next(k for k in (3, 2, 1) if count % k == 0)

    def at_of(place_ref):
        return {"unit": place_ref[0], "near": place_ref[1], "near_next": place_ref[1] + 2}

    def act_spec(which):
        def at(s, place_ref, _):
            return (0, at_of(place_ref)[which])

        return pl.BlockSpec((tok, rows * block), at)

    chunks = [chunk for hid in hids for chunk in hid]
    accs = [] if acc is None else [acc]
    unit_spec = pl.BlockSpec((step_rows * per_row, block, block), lambda s, *_: (s, 0, 0))
    acc_spec = pl.BlockSpec(
        (step_rows * per_row, block, block), lambda s, *_: (first_row // step_rows + s, 0, 0)
    )
    kept = count * per_row
    return pl.pallas_call(
        functools.partial(
            weight_term_kernel, per_row, rows, first_row, grad_scale, len(acts), len(chunks)
        ),
        out_shape=jax.ShapeDtypeStruct((kept, block, block), kind),
        grid_spec=pltpu.PrefetchScalarGridSpec(
            num_scalar_prefetch=2,
            grid=(count // step_rows,),
            in_specs=[act_spec(entry[1]) for entry in acts]
            + [pl.BlockSpec(chunk.shape, lambda s, *_: (0, 0)) for chunk in chunks]
            + [acc_spec] * len(accs),
            out_specs=unit_spec,
        ),
        cost_estimate=pl.CostEstimate(
            flops=2 * kept * len(hids) * tok * block * block,
            bytes_accessed=2 * len(hids) * tok * chunks[0].shape[1] + 8 * kept * block * block,
            transcendentals=0,
        ),
        name="weight_terms",
    )(place, cols, *[entry[0] for entry in acts], *chunks, *accs)


def act_kernel(per_row, rows, set_count, hid_count, place_ref, cols_ref, *refs):
    hid_refs = refs[:hid_count]
    sources = refs[hid_count : hid_count + 2]
    outs = refs[hid_count + 2 : -2]
    held, sems = refs[-2:]
    unit = pl.program_id(0)
    block = held.shape[-1]
    near = jnp.where(unit == 0, place_ref[2], 1 - place_ref[2])

    def copy_of(source, into):
        return pltpu.make_async_copy(source, held.at[into], sems.at[into])

    @pl.when(unit == 0)
    def _():
        for index, source in enumerate(sources):
            @pl.when(place_ref[2] == place_ref[1])
            def _():
                copy_of(source, index).start()

            @pl.when(place_ref[2] != place_ref[1])
            def _():
                copy_of(source, 1 - index).start()

    copy_of(sources[0], unit).wait()

    @pl.loop(0, rows)
    def _(row):
        first = ((place_ref[0] + NEAR * near) * rows + row) * per_row
        hid = columns_of(hid_refs, spans_of(cols_ref, first, per_row, block))
        weight = jnp.concatenate([held[unit, row * per_row + k] for k in range(per_row)], axis=1)
        part = lax.dot_general(
            hid, weight, (((1,), (1,)), ((), ())), preferred_element_type=jnp.float32
        ).astype(jnp.bfloat16)
        tok = part.shape[0] // set_count
        lanes = pl.ds(pl.multiple_of(row * block, block), block)

        @pl.when(unit == 0)
        def _():
            for k in range(set_count):
                outs[2 * k][:, lanes] = part[k * tok : (k + 1) * tok]

        @pl.when(unit == 1)
        def _():
            for k in range(set_count):
                outs[2 * k + 1][:, lanes] = part[k * tok : (k + 1) * tok]


def act_partials(place, cols, hids, weights, rows, per_row):
    block = weights[0].shape[-1]
    chunks = [chunk for hid in hids for chunk in hid]
    tok = sum(chunk.shape[0] for chunk in hids[0])
    out = pl.BlockSpec((tok, rows * block), lambda s, *_: (0, 0))
    shape = jax.ShapeDtypeStruct((tok, rows * block), jnp.bfloat16)
    kept = 2 * rows * per_row
    return pl.pallas_call(
        functools.partial(act_kernel, per_row, rows, len(hids), len(chunks)),
        out_shape=(shape,) * (2 * len(hids)),
        grid_spec=pltpu.PrefetchScalarGridSpec(
            num_scalar_prefetch=2,
            grid=(2,),
            in_specs=[pl.BlockSpec(chunk.shape, lambda s, *_: (0, 0)) for chunk in chunks]
            + [pl.BlockSpec(memory_space=pl.ANY)] * 2,
            out_specs=[out] * (2 * len(hids)),
            scratch_shapes=[
                pltpu.VMEM((2, rows * per_row, block, block), jnp.bfloat16),
                pltpu.SemaphoreType.DMA((2,)),
            ],
        ),
        cost_estimate=pl.CostEstimate(
            flops=2 * kept * len(hids) * tok * block * block,
            bytes_accessed=2 * len(hids) * tok * chunks[0].shape[1] + 2 * kept * block * block,
            transcendentals=0,
        ),
        name="act_partials",
    )(place, cols, *chunks, *weights)


def put_kernel(count, place_ref, *refs):
    ins, out_ref, sems = refs[:count], refs[-2], refs[-1]
    copies = []
    for index, ref in enumerate(ins):
        tok, span = ref.shape
        into = out_ref.at[
            pl.ds(pl.multiple_of(place_ref[count + index] * tok, tok), tok),
            pl.ds(pl.multiple_of(place_ref[index] * span, span), span),
        ]
        copies.append(pltpu.make_async_copy(ref, into, sems.at[index]))
        copies[-1].start()
    for copy in copies:
        copy.wait()


def put_units(units, parts, arrays, whole, shape):
    given = [] if whole is None else [whole]
    count = len(arrays)
    return pl.pallas_call(
        functools.partial(put_kernel, count),
        out_shape=jax.ShapeDtypeStruct(shape, jnp.bfloat16),
        grid_spec=pltpu.PrefetchScalarGridSpec(
            num_scalar_prefetch=1,
            grid=(1,),
            in_specs=[pl.BlockSpec(array.shape, lambda s, *_: (0, 0)) for array in arrays]
            + [pl.BlockSpec(memory_space=pl.ANY)] * len(given),
            out_specs=pl.BlockSpec(memory_space=pl.ANY),
            scratch_shapes=[pltpu.SemaphoreType.DMA((count,))],
        ),
        input_output_aliases={count + 1: 0} if given else {},
        cost_estimate=pl.CostEstimate(
            flops=0, bytes_accessed=4 * count * arrays[0].size, transcendentals=0
        ),
        name="put_units",
    )(jnp.stack(units + parts).astype(jnp.int32), *arrays, *given)


def add_kernel(sum_ref, part_ref, *refs):
    refs[-1][...] = (sum_ref[...] + part_ref[...].astype(jnp.float32)).astype(jnp.bfloat16)


def add_part(total, part, index, size, whole):
    steps = part.shape[0] // size
    given = [] if whole is None else [whole]
    shape = (size, *total.shape[1:])
    at = pl.BlockSpec(shape, lambda s: (index * steps + s, 0, 0))
    return pl.pallas_call(
        add_kernel,
        out_shape=jax.ShapeDtypeStruct(total.shape, jnp.bfloat16),
        grid=(steps,),
        in_specs=[at, pl.BlockSpec(shape, lambda s: (s, 0, 0))]
        + [pl.BlockSpec(memory_space=pl.ANY)] * len(given),
        out_specs=at,
        input_output_aliases={2: 0} if given else {},
        cost_estimate=pl.CostEstimate(
            flops=part.size, bytes_accessed=8 * part.size, transcendentals=0
        ),
        name="add_part",
    )(total, part, *given)


def add_up(left, right):
    return (left.astype(jnp.float32) + right.astype(jnp.float32)).astype(jnp.bfloat16)


def after(value, *others):
    return lax.optimization_barrier((value, *others))[0]


def local_bits(*arrays):
    return local_bits_body(*arrays)


def local_bits_body(activations, pre_act, grad_act, kept_weight, block_cols):
    block = kept_weight.shape[-1]
    tok, width = activations.shape
    dp_size, tensor_size = lax.axis_size("dp"), lax.axis_size("tensor")
    kept = kept_weight.shape[1]
    cols = block_cols[0]
    per_row = cols.shape[0] // (width // block)
    rows = kept // per_row
    span = rows * block
    grad_scale = 1.0 / math.sqrt(tok * dp_size)
    place = lax.axis_index("dp")
    near = (place // NEAR) % 2
    t_place = lax.axis_index("tensor")
    core = t_place % 2

    def swap(value, bits):
        return lax.ppermute(value, "dp", [(d, d ^ bits) for d in range(dp_size)])

    def partner(value, bit):
        return lax.ppermute(value, "tensor", [(t, t ^ bit) for t in range(tensor_size)])

    share = tok // tensor_size

    def share_of(bits, *others):
        mine = after(activations, *others)
        parts = [
            lax.dynamic_slice(
                mine,
                (t_place * share, (((place ^ bits) & (FAR | SIDE)) + NEAR * j) * span),
                (share, span),
            )
            for j in (0, 1)
        ]
        return swap(jnp.concatenate(parts, axis=1), bits)

    def gathered(parts, *others):
        pieces = {0: jnp.concatenate([after(part, *others) for part in parts], axis=1)}
        bit = tensor_size // 2
        while bit:
            held = sorted(pieces)
            joined = jnp.concatenate([pieces[k] for k in held], axis=0)
            got = partner(joined, bit)
            for index, k in enumerate(held):
                pieces[k ^ bit] = got[index * share : (index + 1) * share]
            bit //= 2
        whole = jnp.zeros((tok, pieces[0].shape[1]), activations.dtype)
        for k, value in pieces.items():
            whole = lax.dynamic_update_slice_in_dim(whole, value, (t_place ^ k) * share, 0)
        return whole

    hid_own, hid_side, hid_far = [], [], []
    cut = 0
    for index, part in enumerate(CHUNKS):
        rows_of = slice(cut, cut + part * tok // sum(CHUNKS))
        cut = rows_of.stop
        if hid_own:
            pre_act = after(pre_act, hid_own[-1])
        hid_own.append(hidden_gradient(pre_act[rows_of], grad_act[rows_of]))
        if index < 2:
            hid_far.append(swap(hid_own[index], FAR))
        hid_side.append(swap(hid_own[-1], SIDE))

    side_acts = gathered([share_of(SIDE, hid_own[1])])
    far_shares = [share_of(FAR, hid_own[1]), share_of(FAR | SIDE, hid_own[1])]
    own_weight = kept_weight[0]
    near_weight = swap(after(own_weight, hid_own[-1]), NEAR)

    near_place = jnp.stack([place ^ NEAR, 1 - near]).astype(jnp.int32)
    own_place = jnp.stack([place, near]).astype(jnp.int32)
    act_place = jnp.stack([place & (FAR | SIDE), near, core]).astype(jnp.int32)
    terms = functools.partial(
        weight_terms, cols=cols, rows=rows, per_row=per_row, block=block, grad_scale=grad_scale
    )
    first_terms = functools.partial(
        terms,
        acts=[(activations, "unit"), (side_acts, "near")],
        hids=[hid_own, hid_side],
        acc=None,
        first_row=0,
        count=rows,
        kind=jnp.float32,
    )
    weights = (own_weight, near_weight)

    def acts_of(hids, *others):
        return act_partials(after(act_place, *others), cols, hids, weights, rows, per_row)

    def core_sum(keep, give):
        return add_up(keep, partner(give, 1))

    def more_sum(value):
        bit = 4
        while bit < tensor_size:
            value = add_up(value, partner(value, bit))
            bit *= 2
        return value

    turn = (t_place // 2) % 2
    token_half = tok // 2

    def half_of(value, which):
        return lax.dynamic_slice_in_dim(value, which * token_half, token_half, 0)

    hid_both = [swap(hid_far[0], SIDE)]
    hid_far.append(swap(after(hid_own[2], hid_far[0]), FAR))
    hid_both.append(swap(hid_far[1], SIDE))
    hid_far.append(swap(after(hid_own[3], hid_far[1]), FAR))
    near_sum = first_terms(after(near_place, hid_far[1]))
    own_sum = first_terms(after(own_place, near_sum))
    far_acts = gathered(far_shares, own_sum)
    third = after(hid_far[2], own_sum)
    hid_both.append(swap(third, SIDE))
    parts = acts_of([hid_own, hid_side], third)
    near_cores = [core_sum(parts[0], parts[1]), core_sum(parts[2], parts[3])]
    near_got = [partner(value, 2) for value in near_cores]
    fourth = after(hid_far[3], far_acts, *near_cores)
    hid_both.append(swap(fourth, SIDE))
    parts = acts_of([hid_far], fourth)
    far_core = core_sum(parts[0], parts[1])
    far_got = partner(half_of(far_core, 1 - turn), 2)

    cuts = 2 if rows % 2 == 0 else 1
    came, last = [], far_core
    there = dict(hids=[hid_far, hid_both])
    for k in range(cuts):
        last = terms(
            after(near_place, last),
            acts=[(far_acts, "near"), (far_acts, "near_next")],
            acc=near_sum,
            first_row=k * (rows // cuts),
            count=rows // cuts,
            kind=jnp.bfloat16,
            **there,
        )
        came.append(swap(last, NEAR))
    far_sum = more_sum(add_up(after(half_of(far_core, turn), last), far_got))
    far_back = swap(far_sum, FAR)
    parts = acts_of([hid_both], far_sum)
    both_core = core_sum(parts[0], parts[1])
    both_got = partner(half_of(both_core, 1 - turn), 2)
    own_sum = terms(
        after(own_place, both_core),
        acts=[(far_acts, "near"), (far_acts, "near_next")],
        acc=own_sum,
        first_row=0,
        count=rows,
        kind=jnp.float32,
        **there,
    )
    both_sum = more_sum(add_up(after(half_of(both_core, turn), own_sum), both_got))
    both_back = swap(both_sum, FAR | SIDE)
    halves = [
        more_sum(add_up(after(value, both_sum), got)) for value, got in zip(near_cores, near_got)
    ]
    unit = (place & (FAR | SIDE)) + NEAR * core
    mine = [halves[0], swap(halves[1], SIDE)]

    def put(bits_of, arrays, parts_of, whole):
        there_units = [unit ^ bits for bits in bits_of]
        return put_units(
            there_units + [u ^ NEAR for u in there_units],
            parts_of * 2,
            arrays + [partner(value, 1) for value in arrays],
            whole,
            activations.shape,
        )

    weight_grad = add_part(own_sum, after(came[0], *halves), 0, per_row, None)
    zero = core * 0
    near_put = put([0, SIDE], mine, [zero, zero], None)
    far_back = after(far_back, weight_grad, near_put)
    far_got = partner(far_back, 2)
    both_back = after(both_back, far_back)
    both_got = partner(both_back, 2)
    for k in range(1, cuts):
        weight_grad = add_part(own_sum, after(came[k], both_back), k, per_row, weight_grad)
    act_grad = put(
        [FAR, FAR, FAR | SIDE, FAR | SIDE],
        [far_back, after(far_got, weight_grad), both_back, after(both_got, weight_grad)],
        [turn, 1 - turn] * 2,
        near_put,
    )
    return (weight_grad[None], act_grad)


def fits_bits(mesh, activations, kept_weight):
    dp_size, tensor_size = mesh.shape["dp"], mesh.shape["tensor"]
    block = kept_weight.shape[-1]
    kept_all = kept_weight.shape[1]
    per_row = kept_all // (activations.shape[1] // block)
    return (
        dp_size == 2 * FAR
        and tensor_size >= 4
        and tensor_size & (tensor_size - 1) == 0
        and kept_all % (dp_size * per_row) == 0
        and activations.shape[0] % (dp_size * tensor_size * 16) == 0
        and activations.shape[0] % (dp_size * sum(CHUNKS) * 16) == 0
        and activations.shape[0] // dp_size <= 512
    )


def solution(mesh):
    def whole(activations, pre_act, grad_act, kept_weight, block_cols):
        fits = fits_bits(mesh, activations, kept_weight)
        return jax.shard_map(
            local_bits if fits else local_any,
            mesh=mesh,
            in_specs=(
                P("dp", None),
                P("dp", "tensor"),
                P("dp", "tensor"),
                P("tensor", "dp", None, None),
                P("tensor", None),
            ),
            out_specs=(P("tensor", "dp", None, None), P("dp", None)),
            check_vma=False,
        )(activations, pre_act, grad_act, kept_weight, block_cols)

    return whole
```
